32 devices in a mesh: job: 2 (over y), tile: 4 (over z), src: 4 (over x, core).
Axes of the slice: x: 2, y: 2, z: 4, core: 2. Of those that a mesh axis runs over, the one named last changes fastest.
Arguments:
- forward_field: float32 [8, 2, 16, 256, 128], P(('job', 'src'), None, 'tile'), parts along dimension 0, may hold values from -6 to 6
- adjoint_guess: float32 [8, 2, 16, 256, 128], P(('job', 'src'), None, 'tile'), parts along dimension 0, may hold values from -6 to 6
- conductivity: float32 [32, 256, 128], P(('job', 'tile')), parts along dimension 0, may hold values from 0.3 to 3
- freq_kappa: float32 [8], P('job'), parts along dimension 0, may hold values from 0.5 to 4
- pair_freq: int32 [8], P(('job', 'src')), parts along dimension 0, may hold values from 0 to 3
- recv_data: float32 [8, 2, 256], P(('job', 'src')), parts along dimension 0, may hold values from -6 to 6
- recv_weights: float32 [512, 64], P('job'), parts along dimension 0, may hold values from 0.05 to 1
- recv_x: int32 [512], P('job'), parts along dimension 0, may hold values from 0 to 12
- recv_y: int32 [512], P('job'), parts along dimension 0, may hold values from 0 to 252
- recv_z: int32 [512], P('job'), parts along dimension 0, may hold values from 0 to 124
Outputs:
- adjoint: float32 [8, 2, 16, 256, 128], P(('job', 'src'), None, 'tile'), parts along dimension 0
- gradient: float32 [32, 256, 128], P(('job', 'tile'), 'src'), parts along dimension 0
The draws below stay inside these ranges and needn't reach their ends.
There are 2 independent parts, one for each index of `job`. The reference program is written for one: setup_inputs(seed, part) draws one part's arguments, and reference() takes and returns one part's arrays. A program takes and returns all parts, laid end to end along the dimension named above; each array names one. Nothing has to cross between parts.
Inputs may be any that keep to these rules, and one draw needn't show every extreme that they name: `recv_x`: each receiver's block of 4 x 4 x 4 cells lies inside the grid along the first dimension. `recv_y`: each receiver's block lies inside the grid along the second dimension. `recv_z`: each receiver's block lies inside the grid along the third dimension. `pair_freq`: an index into freq_kappa.
All inputs are finite; a program needn't handle non-finite values.
Results may differ from the reference program's by a relative error of at most 0.00011.
Values sent between devices are 32-bit elements; how exact they have to be, the bound alone decides.
No kernel may reach another device: no remote copies, remote signals or barrier semaphores. Data moves between devices by JAX's collectives and lax.ppermute only.
A program may use at most 64 MiB of HBM per device.

```python
import math
import jax
import jax.numpy as jnp
from jax import lax

NY = 256
NZ = 128
RECV = 256
NF = 4
NX = 16
PAIRS = 4


def place_ends(values, stream_key, smallest, high):
    extent = values.shape
    spot = [jax.random.randint(jax.random.fold_in(stream_key, axis), (), 0, extent[axis]) for axis in range(len(extent))]
    values = values.at[tuple(spot)].set(smallest)
    longest = extent.index(max(extent))
    spot[longest] = (spot[longest] + 1) % extent[longest]
    return values.at[tuple(spot)].set(high)


def shard_levels(rng, shape, cuts, smallest, largest):
    def one(position, shards_of):
        draws = jax.random.uniform(jax.random.fold_in(jax.random.fold_in(rng, 6), position), (shards_of,), jnp.float32, smallest / len(cuts), largest / len(cuts))
        return jnp.repeat(jnp.exp(draws), shape[position] // shards_of).reshape((-1,) + (1,) * (len(shape) - position - 1))

    factor_of = one(*cuts[0])
    for cut in cuts[1:]:
        factor_of = factor_of * one(*cut)
    return factor_of


def gaussian(stream_key, extent, spread, reach, pieces=(), kind=jnp.bfloat16):
    level = shard_levels(stream_key, extent, pieces, -0.22, 0.18) if pieces else 1.0
    drawn = jax.random.normal(stream_key, extent, jnp.float32) * spread * level
    return jnp.minimum(jnp.maximum(drawn, -reach), reach).astype(kind)


def setup_inputs(seed: int = 0, part: int = 0) -> dict:
    key_of = jax.random.split(jax.random.key(seed), 11)
    part_splits = jax.random.split(jax.random.fold_in(key_of[10], part), 11)
    forward_field = gaussian(part_splits[0], (PAIRS, 2, NX, NY, NZ), 1.0, 6.0, ((0, 4), (2, 4)), jnp.float32)
    adjoint_guess = gaussian(part_splits[1], (PAIRS, 2, NX, NY, NZ), 1.0, 6.0, ((0, 4), (2, 4)), jnp.float32)
    conductivity = jnp.clip(jnp.exp(math.log(3.0) - 2.3025851 * jax.random.uniform(part_splits[2], (NX, NY, NZ), jnp.float32) ** shard_levels(part_splits[2], (NX, NY, NZ), ((0, 4),), -0.2, 0.2)), 0.3, 3.0)
    freq_kappa = jnp.clip(jnp.exp(jax.random.uniform(part_splits[3], (NF,), jnp.float32, math.log(0.5), math.log(4.0))), 0.5, 4.0)
    pair_freq = place_ends(jax.random.randint(part_splits[4], (PAIRS,), 0, NF), jax.random.fold_in(part_splits[4], 1), 0, NF - 1).astype(jnp.int32)
    recv_data = gaussian(part_splits[5], (PAIRS, 2, RECV), 1.0, 6.0, ((0, 4),), jnp.float32)
    recv_weights = jnp.clip(jax.random.uniform(part_splits[6], (RECV, 64), jnp.float32, 0.05, 1.0), 0.05, 1.0)
    recv_x = place_ends(jax.random.randint(part_splits[7], (RECV,), 0, NX - 3), jax.random.fold_in(part_splits[7], 1), 0, (NX - 3) - 1).astype(jnp.int32)
    recv_y = place_ends(jax.random.randint(part_splits[8], (RECV,), 0, NY - 3), jax.random.fold_in(part_splits[8], 1), 0, (NY - 3) - 1).astype(jnp.int32)
    recv_z = place_ends(jax.random.randint(part_splits[9], (RECV,), 0, NZ - 3), jax.random.fold_in(part_splits[9], 1), 0, (NZ - 3) - 1).astype(jnp.int32)
    return dict(forward_field=forward_field, adjoint_guess=adjoint_guess, conductivity=conductivity, freq_kappa=freq_kappa, pair_freq=pair_freq, recv_data=recv_data, recv_weights=recv_weights, recv_x=recv_x, recv_y=recv_y, recv_z=recv_z)


def half_sweep(field, source, coupling, denominator, update_mask):
    padded = jnp.pad(field, ((0, 0), (1, 1), (1, 1), (1, 1)))
    beside_all = padded[:, 2:, 1:-1, 1:-1] + padded[:, :-2, 1:-1, 1:-1]
    beside_all = beside_all + padded[:, 1:-1, 2:, 1:-1] + padded[:, 1:-1, :-2, 1:-1]
    beside_all = beside_all + padded[:, 1:-1, 1:-1, 2:] + padded[:, 1:-1, 1:-1, :-2]
    sums = source + beside_all
    real_part = (6.0 * sums[0] + coupling * sums[1]) / denominator
    imag_part = (6.0 * sums[1] - coupling * sums[0]) / denominator
    return jnp.where(update_mask[None], jnp.stack([real_part, imag_part]), field)


def reference(forward_field, adjoint_guess, conductivity, freq_kappa, pair_freq, recv_data, recv_weights, recv_x, recv_y, recv_z):
    offsets = jnp.arange(64, dtype=jnp.int32)
    cell_x = recv_x[:, None] + offsets[None, :] // 16
    cell_y = recv_y[:, None] + (offsets[None, :] // 4) % 4
    cell_z = recv_z[:, None] + offsets[None, :] % 4
    flat_index = ((cell_x * NY + cell_y) * NZ + cell_z).reshape(-1).astype(jnp.int32)
    grid_x = jnp.arange(NX, dtype=jnp.int32)[:, None, None]
    grid_y = jnp.arange(NY, dtype=jnp.int32)[None, :, None]
    grid_z = jnp.arange(NZ, dtype=jnp.int32)[None, None, :]
    colours = (grid_x + grid_y + grid_z) % 2

    def one_pair(total, items):
        forward, guess, residual, freq_index = items
        kappa = freq_kappa[freq_index]
        values = (residual[:, :, None] * recv_weights[None]).reshape(2, -1)
        source = jnp.zeros((2, NX * NY * NZ), jnp.float32).at[:, flat_index].add(values).reshape(2, NX, NY, NZ)
        coupling = kappa * conductivity
        denominator = 36.0 + coupling * coupling
        field = guess
        for colour in (0, 1, 0, 1):
            field = half_sweep(field, source, coupling, denominator, colours == colour)
        total = total + kappa * (forward[0] * field[1] + forward[1] * field[0])
        return total, field

    total, adjoint = lax.scan(one_pair, jnp.zeros((NX, NY, NZ), jnp.float32), (forward_field, adjoint_guess, recv_data, pair_freq))
    return adjoint, -conductivity * total
```

```python
import functools

import jax
import jax.numpy as jnp
from jax import lax
from jax.experimental import pallas as pl
from jax.experimental.pallas import tpu as pltpu
from jax.sharding import PartitionSpec as P

SWEEPS = 4
COLOURS = tuple(k % 2 for k in range(SWEEPS))
HALO_CELLS = tuple(
    (d, c)
    for d in range(1, SWEEPS)
    for c in (0, 1)
    if any(COLOURS[k] == c and d <= SWEEPS - 1 - k for k in range(SWEEPS))
)
PAD = 8
ROWS = 32
UNROLL = 8
SMEM = pl.BlockSpec(memory_space=pltpu.SMEM)
VMEM = pl.BlockSpec(memory_space=pltpu.VMEM)


def odd_lanes(shift, rows, cols):
    return ((lax.broadcasted_iota(jnp.int32, (rows, cols), 1) + shift) & 1) == 1


def of_colour(colour, odd, even_rows, odd_rows):
    if colour == 0:
        return jnp.where(odd, odd_rows, even_rows)
    return jnp.where(odd, even_rows, odd_rows)


def kappa_of(kappa_ref, freq_ref):
    return kappa_ref[freq_ref[0]]


def coefficients(kappa, conductivity):
    coupling = kappa * conductivity
    inverse = 1.0 / (36.0 + coupling * coupling)
    return 6.0 * inverse, coupling * inverse


def pack_kernel(guess_ref, cond_ref, adj_ref, even_ref, odd_ref):
    layers, size_y, size_z = cond_ref.shape
    half = size_y // 2
    rows = min(ROWS, half)
    tile = lax.axis_index("tile")
    first = tile * layers

    for i, (d, c) in enumerate(HALO_CELLS):
        for ref, to_right in ((even_ref, tile % 2 == 0), (odd_ref, tile % 2 == 1)):
            layer = jnp.where(to_right, layers - d, d - 1)
            odd = odd_lanes(first + layer, rows, size_z)
            for r in range(0, half, rows):
                a = cond_ref[layer, pl.ds(2 * r, rows, stride=2), :]
                b = cond_ref[layer, pl.ds(2 * r + 1, rows, stride=2), :]
                ref[i, pl.ds(r, rows), :] = of_colour(c, odd, a, b)
    for layer in range(layers):
        odd = odd_lanes(first + layer, rows, size_z)
        for part in range(2):
            for r in range(0, half, rows):
                a = guess_ref[0, part, layer, pl.ds(2 * r, rows, stride=2), :]
                b = guess_ref[0, part, layer, pl.ds(2 * r + 1, rows, stride=2), :]
                adj_ref[part, layer, pl.ds(r, rows), :] = of_colour(1, odd, a, b)


def source_kernel(
    x_ref, y_ref, z_ref, kappa_ref, freq_ref, weight_ref, data_ref, cond_ref,
    source_ref, six_ref, cross_ref, terms_ref, total_ref,
):
    layers, size_y, size_z = cond_ref.shape
    half = size_y // 2
    rows = min(ROWS, half)
    taps, count = weight_ref.shape
    reach = source_ref.shape[2]
    halo = SWEEPS - 1
    first = lax.axis_index("tile") * layers
    kappa = kappa_of(kappa_ref, freq_ref)

    blank = jnp.zeros((size_z - taps, count), jnp.float32)
    weights = weight_ref[...]
    for c in range(2):
        terms = jnp.concatenate([weights * data_ref[0, c : c + 1, :], blank], axis=0).T
        for b in range(4):
            moved = pltpu.roll(terms, size_z - 4 * b, 1) if b else terms
            terms_ref[pl.ds(2 * b + c, count, stride=8), :] = moved
    for layer in range(reach):
        total_ref[4 + layer] = jnp.zeros(total_ref.shape[1:], jnp.float32)

    lane = lax.broadcasted_iota(jnp.int32, (8, size_z), 1)
    def add_block(r):
        z = z_ref[r]
        base = jnp.clip(x_ref[r] - first + halo, -4, reach) + 4
        row = 2 * y_ref[r]
        inside = (lane - z).astype(jnp.uint32) < 4
        both = terms_ref[pl.ds(pl.multiple_of(8 * r, 8), 8), :]
        terms = []
        for a in range(4):
            moved = pltpu.roll(both, lax.rem(z + size_z - 16 * a, size_z), 1)
            terms.append(jnp.where(inside, moved, 0.0))
        old = [total_ref[base + a, pl.ds(row, 8), :] for a in range(4)]
        for a in range(4):
            total_ref[base + a, pl.ds(row, 8), :] = old[a] + terms[a]

    def some_blocks(step, carry):
        for u in range(UNROLL):
            add_block(step * UNROLL + u)
        return carry

    lax.fori_loop(0, count // UNROLL, some_blocks, 0)

    for layer in range(layers):
        odd = odd_lanes(first + layer, rows, size_z)
        for r in range(0, half, rows):
            a = cond_ref[layer, pl.ds(2 * r, rows, stride=2), :]
            b = cond_ref[layer, pl.ds(2 * r + 1, rows, stride=2), :]
            for c in (0, 1):
                six, cross = coefficients(kappa, of_colour(c, odd, a, b))
                six_ref[c, layer, pl.ds(r, rows), :] = six
                cross_ref[c, layer, pl.ds(r, rows), :] = cross

    def pack_layer(layer, carry):
        odd = odd_lanes(first + layer - halo, rows, size_z)
        for part in range(2):
            for r in range(0, half, rows):
                a = total_ref[4 + layer, pl.ds(4 * r + part, rows, stride=4), :]
                b = total_ref[4 + layer, pl.ds(4 * r + 2 + part, rows, stride=4), :]
                for c in (0, 1):
                    source_ref[c, part, layer, pl.ds(r, rows), :] = of_colour(c, odd, a, b)
        return carry

    lax.fori_loop(0, reach, pack_layer, 0)


def sweep_kernel(
    kappa_ref, freq_ref, adj_ref, adj_even_ref, adj_odd_ref, cond_even_ref, cond_odd_ref,
    source_ref, six_own_ref, cross_own_ref, cond_ref, forward_ref,
    out_ref, send_ref, keep_ref, zero_ref, one_ref, six_ref, cross_ref,
):
    layers, size_y, size_z = cond_ref.shape
    half = size_y // 2
    rows = min(ROWS, half)
    tile = lax.axis_index("tile")
    tiles = lax.axis_size("tile")
    first = tile * layers
    kappa = kappa_of(kappa_ref, freq_ref)
    depth = SWEEPS
    slots = layers + 2 * depth
    packed = (zero_ref, one_ref)

    edge = jnp.zeros((PAD, size_z), jnp.float32)
    for ref in packed:
        for part in range(2):
            for slot in range(slots):
                ref[part, slot, pl.ds(0, PAD), :] = edge
                ref[part, slot, pl.ds(PAD + half, PAD), :] = edge
    for part in range(2):
        for layer in range(layers):
            one_ref[part, depth + layer, pl.ds(PAD, half), :] = adj_ref[part, layer]
    for c in (0, 1):
        for layer in range(layers):
            six_ref[c, depth + layer] = six_own_ref[c, layer]
            cross_ref[c, depth + layer] = cross_own_ref[c, layer]
    for near, cells, on_right in (
        (adj_even_ref, cond_even_ref, tile % 2 == 0),
        (adj_odd_ref, cond_odd_ref, tile % 2 == 1),
    ):
        base = jnp.where(on_right, depth + layers, 0)
        there = jnp.where(jnp.where(on_right, tile < tiles - 1, tile > 0), 1.0, 0.0)
        for part in range(2):
            for layer in range(depth):
                one_ref[part, base + layer, pl.ds(PAD, half), :] = near[part, layer]
        for i, (d, c) in enumerate(HALO_CELLS):
            slot = jnp.where(on_right, depth + layers - 1 + d, depth - d)
            for r in range(0, half, rows):
                six, cross = coefficients(kappa, cells[i, pl.ds(r, rows), :])
                six_ref[c, slot, pl.ds(r, rows), :] = six * there
                cross_ref[c, slot, pl.ds(r, rows), :] = cross * there

    lane = lax.broadcasted_iota(jnp.int32, (rows, size_z), 1)

    def update_layer(c, slot):
        old, new = packed[1 - c], packed[c]
        odd = odd_lanes(first + slot - depth + c, rows, size_z)
        for r in range(0, half, rows):
            sums = []
            for part in range(2):
                here = old[part, slot, pl.ds(PAD + r, rows), :]
                above = old[part, slot, pl.ds(PAD + r + 1, rows), :]
                below = old[part, slot, pl.ds(PAD + r - 1, rows), :]
                total = old[part, slot - 1, pl.ds(PAD + r, rows), :]
                total += old[part, slot + 1, pl.ds(PAD + r, rows), :]
                total += here + jnp.where(odd, above, below)
                total += jnp.where(lane > 0, pltpu.roll(here, 1, 1), 0.0)
                total += jnp.where(lane < size_z - 1, pltpu.roll(here, size_z - 1, 1), 0.0)
                sums.append(total + source_ref[c, part, slot - 1, pl.ds(r, rows), :])
            six = six_ref[c, slot, pl.ds(r, rows), :]
            cross = cross_ref[c, slot, pl.ds(r, rows), :]
            new[0, slot, pl.ds(PAD + r, rows), :] = six * sums[0] + cross * sums[1]
            new[1, slot, pl.ds(PAD + r, rows), :] = six * sums[1] - cross * sums[0]

    for k, c in enumerate(COLOURS):

        def one_layer(slot, carry, c=c):
            update_layer(c, slot)
            return carry

        lax.fori_loop(1 + k, slots - 1 - k, one_layer, 0)

    shards = 2 * send_ref.shape[0]
    shard_rows = size_y // shards
    shard = lax.axis_index("src")
    for layer in range(layers):
        odd = odd_lanes(first + layer, rows, size_z)
        for part in range(2):
            for r in range(0, half, rows):
                a = zero_ref[part, depth + layer, pl.ds(PAD + r, rows), :]
                b = one_ref[part, depth + layer, pl.ds(PAD + r, rows), :]
                out_ref[0, part, layer, pl.ds(2 * r, rows, stride=2), :] = jnp.where(odd, b, a)
                out_ref[0, part, layer, pl.ds(2 * r + 1, rows, stride=2), :] = jnp.where(odd, a, b)

    def one_gradient(layer, carry):
        for m in range(shards):
            ref = send_ref if m % 2 else keep_ref
            start = pl.multiple_of((shard ^ m) * shard_rows, shard_rows)
            at = pl.ds(start, shard_rows)
            products = forward_ref[0, 0, layer, at, :] * out_ref[0, 1, layer, at, :]
            products += forward_ref[0, 1, layer, at, :] * out_ref[0, 0, layer, at, :]
            ref[m // 2, layer] = -cond_ref[layer, at, :] * (kappa * products)
        return carry

    lax.fori_loop(0, layers, one_gradient, 0)


def call(kernel, outs, scratch, specs, out_specs, flops):
    return pl.pallas_call(
        kernel,
        out_shape=[jax.ShapeDtypeStruct(s, jnp.float32) for s in outs],
        in_specs=specs,
        out_specs=out_specs,
        scratch_shapes=[pltpu.VMEM(s, jnp.float32) for s in scratch],
        compiler_params=pltpu.CompilerParams(vmem_limit_bytes=32 << 20),
        cost_estimate=pl.CostEstimate(flops=flops, bytes_accessed=4 << 20, transcendentals=0),
    )


def swap_even(count):
    return [(i, i ^ 1) for i in range(count) if i ^ 1 < count]


def swap_odd(count):
    pairs = [(i, i + 1) for i in range(1, count - 1, 2)]
    return pairs + [(b, a) for a, b in pairs]


def body(
    forward_field,
    adjoint_guess,
    conductivity,
    freq_kappa,
    pair_freq,
    recv_data,
    recv_weights,
    recv_x,
    recv_y,
    recv_z,
):
    pairs, _, layers, size_y, size_z = adjoint_guess.shape
    half = size_y // 2
    count, taps = recv_weights.shape
    tiles = lax.axis_size("tile")
    shards = lax.axis_size("src")
    assert pairs == 1 and layers == SWEEPS and count % UNROLL == 0
    cells = len(HALO_CELLS)
    reach = layers + 2 * (SWEEPS - 1)

    adj, cond_even, cond_odd = call(
        pack_kernel,
        [(2, layers, half, size_z), (cells, half, size_z), (cells, half, size_z)],
        [],
        [VMEM, VMEM],
        [VMEM] * 3,
        1 << 20,
    )(adjoint_guess, conductivity)

    evens, odds = swap_even(tiles), swap_odd(tiles)
    cond_odd = lax.ppermute(cond_odd, "tile", odds)
    cond_even = lax.ppermute(cond_even, "tile", evens)
    adj_odd = lax.ppermute(adj, "tile", odds)
    adj_even = lax.ppermute(adj, "tile", evens)

    source, six, cross = call(
        source_kernel,
        [(2, 2, reach, half, size_z), (2, layers, half, size_z), (2, layers, half, size_z)],
        [(8 * count, size_z), (reach + 8, 2 * size_y, size_z)],
        [SMEM] * 5 + [VMEM] * 3,
        [VMEM] * 3,
        1 << 30,
    )(
        recv_x, recv_y, recv_z, freq_kappa, pair_freq, recv_weights.T, recv_data, conductivity
    )

    slots = layers + 2 * SWEEPS
    shard_rows = size_y // shards
    field, send, keep = call(
        sweep_kernel,
        [
            (1, 2, layers, size_y, size_z),
            (shards // 2, layers, shard_rows, size_z),
            (shards // 2, layers, shard_rows, size_z),
        ],
        [(2, slots, half + 2 * PAD, size_z)] * 2 + [(2, slots, half, size_z)] * 2,
        [SMEM] * 2 + [VMEM] * 10,
        [VMEM] * 3,
        1 << 26,
    )(
        freq_kappa, pair_freq, adj, adj_even, adj_odd, cond_even, cond_odd,
        source, six, cross, conductivity, forward_field,
    )

    bit = 1
    while True:
        swap = [(i, i ^ bit) for i in range(shards)]
        keep = keep + lax.ppermute(send, "src", swap)
        bit *= 2
        if bit == shards:
            break
        send, keep = keep[1::2], keep[0::2]
    return (field, keep[0])


def solution(mesh):
    placed = (
        P(("job", "src"), None, "tile", None, None),
        P(("job", "src"), None, "tile", None, None),
        P(("job", "tile"), None, None),
        P("job"),
        P(("job", "src")),
        P(("job", "src"), None, None),
        P("job", None),
        P("job"),
        P("job"),
        P("job"),
    )
    return jax.shard_map(
        body,
        mesh=mesh,
        in_specs=placed,
        out_specs=(P(("job", "src"), None, "tile", None, None), P(("job", "tile"), "src", None)),
        check_vma=False,
    )
```

```python
import jax
import jax.numpy as jnp
from jax import lax
from jax.experimental import pallas as pl
from jax.experimental.pallas import tpu as pltpu
from jax.sharding import PartitionSpec as P


SWEEPS = 4
COLOURS = tuple(k % 2 for k in range(SWEEPS))
HALO_CELLS = tuple(
    (d, c)
    for d in range(1, SWEEPS)
    for c in (0, 1)
    if any(COLOURS[k] == c and d <= SWEEPS - 1 - k for k in range(SWEEPS))
)
PAD = 8
ROWS = 32
UNROLL = 8
SMEM = pl.BlockSpec(memory_space=pltpu.SMEM)
VMEM = pl.BlockSpec(memory_space=pltpu.VMEM)
HBM = pl.BlockSpec(memory_space=pltpu.HBM)


def odd_lanes(shift, rows, cols):
    return ((lax.broadcasted_iota(jnp.int32, (rows, cols), 1) + shift) & 1) == 1


def of_colour(colour, odd, even_rows, odd_rows):
    if colour == 0:
        return jnp.where(odd, odd_rows, even_rows)
    return jnp.where(odd, even_rows, odd_rows)


def coefficients(kappa, conductivity):
    coupling = kappa * conductivity
    inverse = 1.0 / (36.0 + coupling * coupling)
    return 6.0 * inverse, coupling * inverse


def even_side_on_right():
    return lax.axis_index("tile") % 2 == 0


def layer_of(slot, layers):
    ahead = slot - SWEEPS
    return jnp.where(even_side_on_right(), layers - 1 - ahead, ahead)


def start_all(copies):
    for copy in copies:
        copy.start()
    return copies


def pack_kernel(guess_hbm, cond_hbm, adj_ref, even_ref, odd_ref, guess_ref, cond_ref, sems):
    layers, size_y, size_z = cond_ref.shape
    half = size_y // 2
    shared = even_ref.shape[1]
    rows = min(ROWS, shared)
    first = lax.axis_index("tile") * layers
    cond_copy = pltpu.make_async_copy(cond_hbm, cond_ref, sems.at[0])
    cond_copy.start()
    guess_copies = start_all(
        [
            pltpu.make_async_copy(guess_hbm.at[0, :, i], guess_ref.at[:, i], sems.at[1 + i])
            for i in range(layers)
        ]
    )
    on_right = even_side_on_right()
    offset = lax.axis_index("src") % 2 * shared
    cond_copy.wait()
    for i, (d, c) in enumerate(HALO_CELLS):
        for ref, to_right in ((even_ref, on_right), (odd_ref, jnp.logical_not(on_right))):
            layer = jnp.where(to_right, layers - d, d - 1)
            odd = odd_lanes(first + layer, rows, size_z)
            for r in range(0, shared, rows):
                at = pl.multiple_of(2 * (offset + r), 2 * rows)
                a = cond_ref[layer, pl.ds(at, rows, stride=2), :]
                b = cond_ref[layer, pl.ds(at + 1, rows, stride=2), :]
                ref[i, pl.ds(r, rows), :] = of_colour(c, odd, a, b)
    for layer in range(layers):
        odd = odd_lanes(first + layer, rows, size_z)
        guess_copies[layer].wait()
        for part in range(2):
            for r in range(0, half, rows):
                a = guess_ref[part, layer, pl.ds(2 * r, rows, stride=2), :]
                b = guess_ref[part, layer, pl.ds(2 * r + 1, rows, stride=2), :]
                adj_ref[part, layer, pl.ds(r, rows), :] = of_colour(1, odd, a, b)


def source_kernel(
    x_hbm, y_hbm, z_hbm, kappas_hbm, freq_hbm, weight_hbm, data_hbm, cond_hbm,
    source_ref, six_ref, cross_ref, scale_ref, kappa_ref,
    x_ref, y_ref, z_ref, kappas_ref, freq_ref, weight_ref, data_ref, cond_ref,
    terms_ref, total_ref, sems,
):
    layers, size_y, size_z = cond_ref.shape
    half = size_y // 2
    rows = min(ROWS, half)
    taps, count = weight_ref.shape
    reach = source_ref.shape[2]
    halo = SWEEPS - 1
    first = lax.axis_index("tile") * layers
    copies = start_all(
        [
            pltpu.make_async_copy(a, b, sems.at[i])
            for i, (a, b) in enumerate(
                (
                    (x_hbm, x_ref), (y_hbm, y_ref), (z_hbm, z_ref), (kappas_hbm, kappas_ref),
                    (freq_hbm, freq_ref), (weight_hbm, weight_ref), (data_hbm, data_ref),
                    (cond_hbm, cond_ref),
                )
            )
        ]
    )
    for layer in range(reach):
        total_ref[4 + layer] = jnp.zeros(total_ref.shape[1:], jnp.float32)
    for copy in copies:
        copy.wait()
    kappa = kappas_ref[freq_ref[0]]
    kappa_ref[...] = jnp.full(kappa_ref.shape, kappa, jnp.float32)

    blank = jnp.zeros((size_z - taps, count), jnp.float32)
    weights = weight_ref[...]
    for c in range(2):
        terms = jnp.concatenate([weights * data_ref[0, c : c + 1, :], blank], axis=0).T
        for b in range(4):
            moved = pltpu.roll(terms, size_z - 4 * b, 1) if b else terms
            terms_ref[pl.ds(2 * b + c, count, stride=8), :] = moved

    lane = lax.broadcasted_iota(jnp.int32, (8, size_z), 1)

    def add_block(r):
        z = z_ref[r]
        base = jnp.clip(x_ref[r] - first + halo, -4, reach) + 4
        row = 2 * y_ref[r]
        inside = (lane - z).astype(jnp.uint32) < 4
        both = terms_ref[pl.ds(pl.multiple_of(8 * r, 8), 8), :]
        terms = []
        for a in range(4):
            moved = pltpu.roll(both, lax.rem(z + size_z - 16 * a, size_z), 1)
            terms.append(jnp.where(inside, moved, 0.0))
        old = [total_ref[base + a, pl.ds(row, 8), :] for a in range(4)]
        for a in range(4):
            total_ref[base + a, pl.ds(row, 8), :] = old[a] + terms[a]

    def some_blocks(step, carry):
        for u in range(UNROLL):
            add_block(step * UNROLL + u)
        return carry

    lax.fori_loop(0, count // UNROLL, some_blocks, 0)

    for ahead in range(layers):
        layer = layer_of(SWEEPS + ahead, layers)
        odd = odd_lanes(first + layer, rows, size_z)
        for r in range(0, half, rows):
            a = cond_ref[layer, pl.ds(2 * r, rows, stride=2), :]
            b = cond_ref[layer, pl.ds(2 * r + 1, rows, stride=2), :]
            for c in (0, 1):
                six, cross = coefficients(kappa, of_colour(c, odd, a, b))
                six_ref[c, ahead, pl.ds(r, rows), :] = six
                cross_ref[c, ahead, pl.ds(r, rows), :] = cross
        scale_ref[ahead] = -(kappa * cond_ref[layer])

    def pack_layer(i, carry):
        layer = layer_of(i + 1, layers)
        odd = odd_lanes(first + layer, rows, size_z)
        for part in range(2):
            for r in range(0, half, rows):
                a = total_ref[4 + halo + layer, pl.ds(4 * r + part, rows, stride=4), :]
                b = total_ref[4 + halo + layer, pl.ds(4 * r + 2 + part, rows, stride=4), :]
                for c in (0, 1):
                    source_ref[c, part, i, pl.ds(r, rows), :] = of_colour(c, odd, a, b)
        return carry

    lax.fori_loop(0, reach, pack_layer, 0)


class Sweeper:
    def __init__(self, half, size_z, layers, source, six, cross):
        self.half, self.size_z = half, size_z
        self.source, self.six, self.cross = source, six, cross
        self.where = ({}, {})
        first = lax.axis_index("tile") * layers
        self.rows = min(ROWS, half)
        base = first + jnp.where(even_side_on_right(), layers - 1, 0)
        self.odd = odd_lanes(base, self.rows, size_z)
        lane = lax.broadcasted_iota(jnp.int32, (self.rows, size_z), 1)
        self.after, self.before = lane > 0, lane < size_z - 1
        near = lax.broadcasted_iota(jnp.int32, (size_z, size_z), 0)
        near = jnp.abs(near - lax.broadcasted_iota(jnp.int32, (size_z, size_z), 1)) <= 1
        near = jnp.where(near, 1.0, 0.0).astype(jnp.bfloat16)
        self.near = jnp.concatenate([near] * 3, axis=0)

    def along_z(self, values):
        high = values.astype(jnp.bfloat16)
        rest = values - high.astype(jnp.float32)
        middle = rest.astype(jnp.bfloat16)
        low = (rest - middle.astype(jnp.float32)).astype(jnp.bfloat16)
        pieces = jnp.concatenate([high, middle, low], axis=1)
        return jnp.dot(pieces, self.near, preferred_element_type=jnp.float32)

    def sums(self, c, part, slot):
        old = self.where[1 - c]
        here, left, right = old[slot], old[slot - 1], old[slot + 1]
        rows = self.rows
        by_matrix = part == 1
        if by_matrix:
            beside = self.along_z(here[part, slot, pl.ds(PAD, self.half), :])
        out = []
        for r in range(0, self.half, rows):
            above = here[part, slot, pl.ds(PAD + r + 1, rows), :]
            below = here[part, slot, pl.ds(PAD + r - 1, rows), :]
            if (slot + c) % 2:
                above, below = below, above
            total = left[part, slot - 1, pl.ds(PAD + r, rows), :]
            total += right[part, slot + 1, pl.ds(PAD + r, rows), :]
            total += jnp.where(self.odd, above, below)
            if by_matrix:
                total += beside[r : r + rows]
            else:
                centre = here[part, slot, pl.ds(PAD + r, rows), :]
                total += centre
                total += jnp.where(self.after, pltpu.roll(centre, 1, 1), 0.0)
                total += jnp.where(self.before, pltpu.roll(centre, self.size_z - 1, 1), 0.0)
            out.append(total + self.source[c, part, slot - 1, pl.ds(r, rows), :])
        return out

    def update(self, c, slot, new):
        sums = [self.sums(c, part, slot) for part in range(2)]
        for i, r in enumerate(range(0, self.half, self.rows)):
            six = self.six[c, slot, pl.ds(r, self.rows), :]
            cross = self.cross[c, slot, pl.ds(r, self.rows), :]
            at = pl.ds(PAD + r, self.rows)
            new[0, slot, at, :] = six * sums[0][i] + cross * sums[1][i]
            new[1, slot, at, :] = six * sums[1][i] - cross * sums[0][i]
        self.where[c][slot] = new


def clear_edges(ref, slots, half):
    edge = jnp.zeros((PAD, ref.shape[-1]), jnp.float32)
    for part in range(2):
        for slot in slots:
            ref[part, slot, pl.ds(0, PAD), :] = edge
            ref[part, slot, pl.ds(PAD + half, PAD), :] = edge


def near_kernel(
    adj_ref, even_ref, ce_own_ref, co_own_ref, ce_other_ref, co_other_ref,
    source_ref, six_own_ref, cross_own_ref, kappa_ref,
    zero_ref, one_ref, six_ref, cross_ref,
):
    _, layers, half, size_z = adj_ref.shape
    tile, tiles = lax.axis_index("tile"), lax.axis_size("tile")
    on_right = even_side_on_right()
    shared = ce_own_ref.shape[1]
    rows = min(ROWS, shared)
    reached = layers + SWEEPS
    clear_edges(zero_ref, range(1, reached - 1), half)
    clear_edges(one_ref, range(reached), half)
    for part in range(2):
        for slot in range(reached):
            layer = layer_of(slot, layers)
            if slot < SWEEPS:
                values = even_ref[part, jnp.where(on_right, layer - layers, layer + SWEEPS)]
            else:
                values = adj_ref[part, layer]
            one_ref[part, slot, pl.ds(PAD, half), :] = values
    for c in (0, 1):
        for layer in range(layers):
            six_ref[c, SWEEPS + layer] = six_own_ref[c, layer]
            cross_ref[c, SWEEPS + layer] = cross_own_ref[c, layer]
    kappa = jnp.broadcast_to(kappa_ref[0:1, :], (rows, size_z))
    parity = lax.axis_index("src") % 2
    is_last, is_first = tile == tiles - 1, tile == 0
    for own, other, outer, missing in (
        (ce_own_ref, ce_other_ref, -1, jnp.where(on_right, is_last, is_first)),
        (co_own_ref, co_other_ref, 1, jnp.where(on_right, is_first, is_last)),
    ):
        there = jnp.where(missing, 0.0, 1.0)
        for i, (d, c) in enumerate(HALO_CELLS):
            slot = SWEEPS - d if outer < 0 else SWEEPS + layers - 1 + d
            for ref, start in ((own, parity * shared), (other, (1 - parity) * shared)):
                for r in range(0, shared, rows):
                    six, cross = coefficients(kappa, ref[i, pl.ds(r, rows), :])
                    at = pl.ds(pl.multiple_of(start + r, rows), rows)
                    six_ref[c, slot, at, :] = six * there
                    cross_ref[c, slot, at, :] = cross * there
    sweeper = Sweeper(half, size_z, layers, source_ref, six_ref, cross_ref)
    sweeper.where[1].update({slot: one_ref for slot in range(reached)})
    for k, c in enumerate(COLOURS):
        for slot in range(1 + k, reached - 1 - k):
            sweeper.update(c, slot, (zero_ref, one_ref)[c])


def far_kernel(
    zero_in_ref, one_in_ref, odd_ref, source_ref, six_ref, cross_ref, scale_ref, forward_ref,
    zero_ref, one_ref, send_ref, keep_ref,
):
    _, slots, _, size_z = zero_in_ref.shape
    layers, size_y, _ = scale_ref.shape
    half = size_y // 2
    on_right = even_side_on_right()
    reached = layers + SWEEPS
    clear_edges(zero_ref, range(SWEEPS, slots - 1), half)
    clear_edges(one_ref, range(SWEEPS, slots), half)
    for part in range(2):
        for slot in range(reached, slots):
            layer = layer_of(slot, layers)
            values = odd_ref[part, jnp.where(on_right, layer + SWEEPS, layer - layers)]
            one_ref[part, slot, pl.ds(PAD, half), :] = values
    sweeper = Sweeper(half, size_z, layers, source_ref, six_ref, cross_ref)
    sweeper.where[0].update({slot: zero_in_ref for slot in range(1, reached - 1)})
    sweeper.where[1].update({slot: one_in_ref for slot in range(reached)})
    sweeper.where[1].update({slot: one_ref for slot in range(reached, slots)})
    for k, c in enumerate(COLOURS):
        for slot in range(reached - 1 - k, slots - 1 - k):
            sweeper.update(c, slot, (zero_ref, one_ref)[c])
    for slot in range(SWEEPS, SWEEPS + layers):
        if sweeper.where[0][slot] is zero_in_ref:
            for part in range(2):
                zero_ref[part, slot, pl.ds(PAD, half), :] = zero_in_ref[part, slot, pl.ds(PAD, half), :]

    shards = 2 * send_ref.shape[0]
    shard = lax.axis_index("src")
    shard_rows = size_y // shards
    rows = min(ROWS, shard_rows // 2)
    for slot in range(SWEEPS, SWEEPS + layers):
        layer = layer_of(slot, layers)
        swap = odd_lanes(lax.axis_index("tile") * layers + layer, rows, size_z)
        for m in range(shards):
            ref = send_ref if m % 2 else keep_ref
            start = (shard ^ m) * shard_rows
            for r in range(0, shard_rows // 2, rows):
                at = pl.ds(pl.multiple_of(PAD + start // 2 + r, PAD), rows)
                a = [zero_ref[part, slot, at, :] for part in range(2)]
                b = [one_ref[part, slot, at, :] for part in range(2)]
                for second in range(2):
                    if second:
                        a, b = b, a
                    field = [jnp.where(swap, b[part], a[part]) for part in range(2)]
                    cells = pl.ds(pl.multiple_of(start + 2 * r, 2 * rows) + second, rows, stride=2)
                    products = forward_ref[0, 0, layer, cells, :] * field[1]
                    products += forward_ref[0, 1, layer, cells, :] * field[0]
                    into = pl.ds(2 * r + second, rows, stride=2)
                    ref[m // 2, layer, into, :] = scale_ref[slot - SWEEPS, cells, :] * products


def unpack_kernel(zero_ref, one_ref, out_hbm, out_ref, sems):
    _, layers, size_y, size_z = out_ref.shape
    half = size_y // 2
    rows = min(ROWS, half)
    first = lax.axis_index("tile") * layers
    copies = []
    for slot in range(SWEEPS, SWEEPS + layers):
        layer = layer_of(slot, layers)
        odd = odd_lanes(first + layer, rows, size_z)
        for part in range(2):
            for r in range(0, half, rows):
                a = zero_ref[part, slot, pl.ds(PAD + r, rows), :]
                b = one_ref[part, slot, pl.ds(PAD + r, rows), :]
                out_ref[part, slot - SWEEPS, pl.ds(2 * r, rows, stride=2), :] = jnp.where(odd, b, a)
                out_ref[part, slot - SWEEPS, pl.ds(2 * r + 1, rows, stride=2), :] = jnp.where(odd, a, b)
        i = slot - SWEEPS
        copies.append(
            pltpu.make_async_copy(out_ref.at[:, i], out_hbm.at[0, :, layer], sems.at[i])
        )
        copies[-1].start()
    for copy in copies:
        copy.wait()


def call(kernel, outs, scratch, specs, out_specs, flops):
    return pl.pallas_call(
        kernel,
        out_shape=[jax.ShapeDtypeStruct(s, jnp.float32) for s in outs],
        in_specs=specs,
        out_specs=out_specs,
        scratch_shapes=scratch,
        compiler_params=pltpu.CompilerParams(vmem_limit_bytes=20 << 20),
        cost_estimate=pl.CostEstimate(flops=flops, bytes_accessed=4 << 20, transcendentals=0),
    )


def floats(*shapes):
    return [pltpu.VMEM(s, jnp.float32) for s in shapes]


def swap_even(count):
    return [(i, i ^ 1) for i in range(count) if i ^ 1 < count]


def swap_odd(count):
    pairs = [(i, i + 1) for i in range(1, count - 1, 2)]
    return pairs + [(b, a) for a, b in pairs]


def body(
    forward_field,
    adjoint_guess,
    conductivity,
    freq_kappa,
    pair_freq,
    recv_data,
    recv_weights,
    recv_x,
    recv_y,
    recv_z,
):
    pairs, _, layers, size_y, size_z = adjoint_guess.shape
    half = size_y // 2
    count, taps = recv_weights.shape
    tiles = lax.axis_size("tile")
    shards = lax.axis_size("src")
    assert pairs == 1 and layers == SWEEPS and count % UNROLL == 0
    cells = len(HALO_CELLS)
    reach = layers + 2 * (SWEEPS - 1)
    slots = layers + 2 * SWEEPS
    evens, odds = swap_even(tiles), swap_odd(tiles)
    flip = [(i, i ^ 1) for i in range(shards)]

    adj, cond_even, cond_odd = call(
        pack_kernel,
        [(2, layers, half, size_z), (cells, half // 2, size_z), (cells, half // 2, size_z)],
        floats((2, layers, size_y, size_z), (layers, size_y, size_z))
        + [pltpu.SemaphoreType.DMA((1 + layers,))],
        [HBM, HBM],
        [VMEM] * 3,
        1 << 20,
    )(adjoint_guess, conductivity)

    cond_even = lax.ppermute(cond_even, "tile", evens)
    cond_odd = lax.ppermute(cond_odd, "tile", odds)
    adj_even = lax.ppermute(adj, "tile", evens)
    adj_odd = lax.ppermute(adj, "tile", odds)

    source, six_own, cross_own, scale, kappa = call(
        source_kernel,
        [
            (2, 2, reach, half, size_z),
            (2, layers, half, size_z),
            (2, layers, half, size_z),
            (layers, size_y, size_z),
            (8, size_z),
        ],
        [pltpu.SMEM((count,), jnp.int32)] * 3
        + [pltpu.SMEM(freq_kappa.shape, jnp.float32), pltpu.SMEM(pair_freq.shape, jnp.int32)]
        + floats(
            (taps, count),
            recv_data.shape,
            (layers, size_y, size_z),
            (8 * count, size_z),
            (reach + 8, 2 * size_y, size_z),
        )
        + [pltpu.SemaphoreType.DMA((8,))],
        [HBM] * 8,
        [VMEM] * 5,
        1 << 30,
    )(
        recv_x, recv_y, recv_z, freq_kappa, pair_freq, recv_weights.T, recv_data, conductivity
    )

    other_even = lax.ppermute(cond_even, "src", flip)
    other_odd = lax.ppermute(cond_odd, "src", flip)

    state = (2, slots, half + 2 * PAD, size_z)
    weights = (2, slots, half, size_z)
    zero, one, six, cross = call(
        near_kernel, [state, state, weights, weights], [], [VMEM] * 10, [VMEM] * 4, 1 << 26
    )(
        adj, adj_even, cond_even, cond_odd, other_even, other_odd,
        source, six_own, cross_own, kappa,
    )

    shard_rows = size_y // shards
    part_shape = (shards // 2, layers, shard_rows, size_z)
    zero, one, send, keep = call(
        far_kernel, [state, state, part_shape, part_shape], [], [VMEM] * 8, [VMEM] * 4, 1 << 26
    )(zero, one, adj_odd, source, six, cross, scale, forward_field)

    (field,) = call(
        unpack_kernel,
        [(1, 2, layers, size_y, size_z)],
        floats((2, layers, size_y, size_z)) + [pltpu.SemaphoreType.DMA((layers,))],
        [VMEM] * 2,
        [HBM],
        1 << 20,
    )(zero, one)

    bit = 1
    while True:
        keep = keep + lax.ppermute(send, "src", [(i, i ^ bit) for i in range(shards)])
        bit *= 2
        if bit == shards:
            break
        send, keep = keep[1::2], keep[0::2]
    return (field, keep[0])


def solution(mesh):
    placed = (
        P(("job", "src"), None, "tile", None, None),
        P(("job", "src"), None, "tile", None, None),
        P(("job", "tile"), None, None),
        P("job"),
        P(("job", "src")),
        P(("job", "src"), None, None),
        P("job", None),
        P("job"),
        P("job"),
        P("job"),
    )
    return jax.shard_map(
        body,
        mesh=mesh,
        in_specs=placed,
        out_specs=(P(("job", "src"), None, "tile", None, None), P(("job", "tile"), "src", None)),
        check_vma=False,
    )
```

```python
import jax
import jax.numpy as jnp
from jax import lax
from jax.experimental import pallas as pl
from jax.experimental.pallas import tpu as pltpu
from jax.sharding import PartitionSpec as P


SWEEPS = 4
COLOURS = tuple(k % 2 for k in range(SWEEPS))
HALO_CELLS = tuple(
    (d, c)
    for d in range(1, SWEEPS)
    for c in (0, 1)
    if any(COLOURS[k] == c and d <= SWEEPS - 1 - k for k in range(SWEEPS))
)
PAD = 8
ROWS = 32
UNROLL = 8
SMEM = pl.BlockSpec(memory_space=pltpu.SMEM)
VMEM = pl.BlockSpec(memory_space=pltpu.VMEM)
HBM = pl.BlockSpec(memory_space=pltpu.HBM)


def odd_lanes(shift, rows, cols):
    return ((lax.broadcasted_iota(jnp.int32, (rows, cols), 1) + shift) & 1) == 1


def of_colour(colour, odd, even_rows, odd_rows):
    if colour == 0:
        return jnp.where(odd, odd_rows, even_rows)
    return jnp.where(odd, even_rows, odd_rows)


def coefficients(kappa, conductivity):
    coupling = kappa * conductivity
    inverse = 1.0 / (36.0 + coupling * coupling)
    return 6.0 * inverse, coupling * inverse


def even_side_on_right():
    return lax.axis_index("tile") % 2 == 0


def layer_of(slot, layers):
    ahead = slot - SWEEPS
    return jnp.where(even_side_on_right(), layers - 1 - ahead, ahead)


def start_all(copies):
    for copy in copies:
        copy.start()
    return copies


def pack_kernel(guess_hbm, cond_hbm, adj_ref, cells_ref, guess_ref, cond_ref, sems):
    layers, size_y, size_z = cond_ref.shape
    half = size_y // 2
    rows = min(ROWS, half)
    first = lax.axis_index("tile") * layers
    cond_copy = pltpu.make_async_copy(cond_hbm, cond_ref, sems.at[0])
    cond_copy.start()
    guess_copies = start_all(
        [
            pltpu.make_async_copy(guess_hbm.at[0, :, i], guess_ref.at[:, i], sems.at[1 + i])
            for i in range(layers)
        ]
    )
    to_right = even_side_on_right() == (lax.axis_index("src") % 2 == 0)
    cond_copy.wait()
    for i, (d, c) in enumerate(HALO_CELLS):
        layer = jnp.where(to_right, layers - d, d - 1)
        odd = odd_lanes(first + layer, rows, size_z)
        for r in range(0, half, rows):
            a = cond_ref[layer, pl.ds(2 * r, rows, stride=2), :]
            b = cond_ref[layer, pl.ds(2 * r + 1, rows, stride=2), :]
            cells_ref[i, pl.ds(r, rows), :] = of_colour(c, odd, a, b)
    for layer in range(layers):
        odd = odd_lanes(first + layer, rows, size_z)
        guess_copies[layer].wait()
        for part in range(2):
            for r in range(0, half, rows):
                a = guess_ref[part, layer, pl.ds(2 * r, rows, stride=2), :]
                b = guess_ref[part, layer, pl.ds(2 * r + 1, rows, stride=2), :]
                adj_ref[part, layer, pl.ds(r, rows), :] = of_colour(1, odd, a, b)


def source_kernel(
    x_hbm, y_hbm, z_hbm, kappas_hbm, freq_ref, weight_hbm, data_hbm, cond_hbm,
    source_ref, six_ref, cross_ref, scale_ref, kappa_ref,
    x_ref, y_ref, z_ref, kappas_ref, weight_ref, data_ref, cond_ref,
    terms_ref, total_ref, sems,
):
    layers, size_y, size_z = cond_ref.shape
    half = size_y // 2
    rows = min(ROWS, half)
    taps, count = weight_ref.shape
    reach = source_ref.shape[2]
    halo = SWEEPS - 1
    first = lax.axis_index("tile") * layers
    copies = start_all(
        [
            pltpu.make_async_copy(a, b, sems.at[i])
            for i, (a, b) in enumerate(
                (
                    (x_hbm, x_ref), (y_hbm, y_ref), (z_hbm, z_ref), (kappas_hbm, kappas_ref),
                    (weight_hbm, weight_ref), (data_hbm, data_ref),
                    (cond_hbm, cond_ref),
                )
            )
        ]
    )
    for layer in range(reach):
        total_ref[4 + layer] = jnp.zeros(total_ref.shape[1:], jnp.float32)
    for copy in copies:
        copy.wait()
    kappa = kappas_ref[freq_ref[0]]
    kappa_ref[...] = jnp.full(kappa_ref.shape, kappa, jnp.float32)

    blank = jnp.zeros((size_z - taps, count), jnp.float32)
    weights = weight_ref[...]
    for c in range(2):
        terms = jnp.concatenate([weights * data_ref[0, c : c + 1, :], blank], axis=0).T
        for b in range(4):
            moved = pltpu.roll(terms, size_z - 4 * b, 1) if b else terms
            terms_ref[pl.ds(2 * b + c, count, stride=8), :] = moved

    lane = lax.broadcasted_iota(jnp.int32, (8, size_z), 1)

    def add_block(r):
        z = z_ref[r]
        base = jnp.clip(x_ref[r] - first + halo, -4, reach) + 4
        row = 2 * y_ref[r]
        inside = (lane - z).astype(jnp.uint32) < 4
        both = terms_ref[pl.ds(pl.multiple_of(8 * r, 8), 8), :]
        terms = []
        for a in range(4):
            moved = pltpu.roll(both, lax.rem(z + size_z - 16 * a, size_z), 1)
            terms.append(jnp.where(inside, moved, 0.0))
        old = [total_ref[base + a, pl.ds(row, 8), :] for a in range(4)]
        for a in range(4):
            total_ref[base + a, pl.ds(row, 8), :] = old[a] + terms[a]

    def some_blocks(step, carry):
        for u in range(UNROLL):
            add_block(step * UNROLL + u)
        return carry

    lax.fori_loop(0, count // UNROLL, some_blocks, 0)

    for ahead in range(layers):
        layer = layer_of(SWEEPS + ahead, layers)
        odd = odd_lanes(first + layer, rows, size_z)
        for r in range(0, half, rows):
            a = cond_ref[layer, pl.ds(2 * r, rows, stride=2), :]
            b = cond_ref[layer, pl.ds(2 * r + 1, rows, stride=2), :]
            for c in (0, 1):
                six, cross = coefficients(kappa, of_colour(c, odd, a, b))
                six_ref[c, ahead, pl.ds(r, rows), :] = six
                cross_ref[c, ahead, pl.ds(r, rows), :] = cross
        scale_ref[ahead] = -(kappa * cond_ref[layer])

    def pack_layer(i, carry):
        layer = layer_of(i + 1, layers)
        odd = odd_lanes(first + layer, rows, size_z)
        for part in range(2):
            for r in range(0, half, rows):
                a = total_ref[4 + halo + layer, pl.ds(4 * r + part, rows, stride=4), :]
                b = total_ref[4 + halo + layer, pl.ds(4 * r + 2 + part, rows, stride=4), :]
                for c in (0, 1):
                    source_ref[c, part, i, pl.ds(r, rows), :] = of_colour(c, odd, a, b)
        return carry

    lax.fori_loop(0, reach, pack_layer, 0)


class Sweeper:
    def __init__(self, half, size_z, layers, source, six, cross):
        self.half, self.size_z = half, size_z
        self.source, self.six, self.cross = source, six, cross
        self.where = ({}, {})
        first = lax.axis_index("tile") * layers
        self.rows = min(ROWS, half)
        base = first + jnp.where(even_side_on_right(), layers - 1, 0)
        self.odd = odd_lanes(base, self.rows, size_z)
        lane = lax.broadcasted_iota(jnp.int32, (self.rows, size_z), 1)
        self.after, self.before = lane > 0, lane < size_z - 1
        near = lax.broadcasted_iota(jnp.int32, (size_z, size_z), 0)
        near = jnp.abs(near - lax.broadcasted_iota(jnp.int32, (size_z, size_z), 1)) <= 1
        near = jnp.where(near, 1.0, 0.0).astype(jnp.bfloat16)
        self.near = jnp.concatenate([near] * 3, axis=0)

    def along_z(self, values):
        high = values.astype(jnp.bfloat16)
        rest = values - high.astype(jnp.float32)
        middle = rest.astype(jnp.bfloat16)
        low = (rest - middle.astype(jnp.float32)).astype(jnp.bfloat16)
        pieces = jnp.concatenate([high, middle, low], axis=1)
        return jnp.dot(pieces, self.near, preferred_element_type=jnp.float32)

    def sums(self, c, part, slot):
        old = self.where[1 - c]
        here, left, right = old[slot], old[slot - 1], old[slot + 1]
        rows = self.rows
        by_matrix = part == 1
        if by_matrix:
            beside = self.along_z(here[part, slot, pl.ds(PAD, self.half), :])
        out = []
        for r in range(0, self.half, rows):
            above = here[part, slot, pl.ds(PAD + r + 1, rows), :]
            below = here[part, slot, pl.ds(PAD + r - 1, rows), :]
            if (slot + c) % 2:
                above, below = below, above
            total = left[part, slot - 1, pl.ds(PAD + r, rows), :]
            total += right[part, slot + 1, pl.ds(PAD + r, rows), :]
            total += jnp.where(self.odd, above, below)
            if by_matrix:
                total += beside[r : r + rows]
            else:
                centre = here[part, slot, pl.ds(PAD + r, rows), :]
                total += centre
                total += jnp.where(self.after, pltpu.roll(centre, 1, 1), 0.0)
                total += jnp.where(self.before, pltpu.roll(centre, self.size_z - 1, 1), 0.0)
            out.append(total + self.source[c, part, slot - 1, pl.ds(r, rows), :])
        return out

    def update(self, c, slot, new):
        sums = [self.sums(c, part, slot) for part in range(2)]
        for i, r in enumerate(range(0, self.half, self.rows)):
            six = self.six[c, slot, pl.ds(r, self.rows), :]
            cross = self.cross[c, slot, pl.ds(r, self.rows), :]
            at = pl.ds(PAD + r, self.rows)
            new[0, slot, at, :] = six * sums[0][i] + cross * sums[1][i]
            new[1, slot, at, :] = six * sums[1][i] - cross * sums[0][i]
        self.where[c][slot] = new


def clear_edges(ref, slots, half):
    edge = jnp.zeros((PAD, ref.shape[-1]), jnp.float32)
    for part in range(2):
        for slot in slots:
            ref[part, slot, pl.ds(0, PAD), :] = edge
            ref[part, slot, pl.ds(PAD + half, PAD), :] = edge


def near_kernel(
    adj_ref, even_ref, cells_ref, other_cells_ref,
    source_ref, six_own_ref, cross_own_ref, kappa_ref,
    zero_ref, one_ref, six_ref, cross_ref,
):
    _, layers, half, size_z = adj_ref.shape
    tile, tiles = lax.axis_index("tile"), lax.axis_size("tile")
    on_right = even_side_on_right()
    rows = min(ROWS, half)
    reached = layers + SWEEPS
    clear_edges(zero_ref, range(1, reached - 1), half)
    clear_edges(one_ref, range(reached), half)
    for part in range(2):
        for slot in range(reached):
            layer = layer_of(slot, layers)
            if slot < SWEEPS:
                values = even_ref[part, jnp.where(on_right, layer - layers, layer + SWEEPS)]
            else:
                values = adj_ref[part, layer]
            one_ref[part, slot, pl.ds(PAD, half), :] = values
    for c in (0, 1):
        for layer in range(layers):
            six_ref[c, SWEEPS + layer] = six_own_ref[c, layer]
            cross_ref[c, SWEEPS + layer] = cross_own_ref[c, layer]
    kappa = jnp.broadcast_to(kappa_ref[0:1, :], (rows, size_z))
    parity = lax.axis_index("src") % 2
    for ref, even_side in ((cells_ref, parity == 0), (other_cells_ref, parity == 1)):
        missing = jnp.where(on_right == even_side, tile == tiles - 1, tile == 0)
        there = jnp.where(missing, 0.0, 1.0)
        for i, (d, c) in enumerate(HALO_CELLS):
            slot = jnp.where(even_side, SWEEPS - d, SWEEPS + layers - 1 + d)
            for r in range(0, half, rows):
                six, cross = coefficients(kappa, ref[i, pl.ds(r, rows), :])
                six_ref[c, slot, pl.ds(r, rows), :] = six * there
                cross_ref[c, slot, pl.ds(r, rows), :] = cross * there
    sweeper = Sweeper(half, size_z, layers, source_ref, six_ref, cross_ref)
    sweeper.where[1].update({slot: one_ref for slot in range(reached)})
    for k, c in enumerate(COLOURS):
        for slot in range(1 + k, reached - 1 - k):
            sweeper.update(c, slot, (zero_ref, one_ref)[c])


def far_kernel(
    zero_in_ref, one_in_ref, odd_ref, source_ref, six_ref, cross_ref, scale_ref, forward_ref,
    zero_ref, one_ref, send_ref, keep_ref,
):
    _, slots, _, size_z = zero_in_ref.shape
    layers, size_y, _ = scale_ref.shape
    half = size_y // 2
    on_right = even_side_on_right()
    reached = layers + SWEEPS
    clear_edges(zero_ref, range(SWEEPS, slots - 1), half)
    clear_edges(one_ref, range(SWEEPS, slots), half)
    for part in range(2):
        for slot in range(reached, slots):
            layer = layer_of(slot, layers)
            values = odd_ref[part, jnp.where(on_right, layer + SWEEPS, layer - layers)]
            one_ref[part, slot, pl.ds(PAD, half), :] = values
    sweeper = Sweeper(half, size_z, layers, source_ref, six_ref, cross_ref)
    sweeper.where[0].update({slot: zero_in_ref for slot in range(1, reached - 1)})
    sweeper.where[1].update({slot: one_in_ref for slot in range(reached)})
    sweeper.where[1].update({slot: one_ref for slot in range(reached, slots)})
    for k, c in enumerate(COLOURS):
        for slot in range(reached - 1 - k, slots - 1 - k):
            sweeper.update(c, slot, (zero_ref, one_ref)[c])
    for slot in range(SWEEPS, SWEEPS + layers):
        if sweeper.where[0][slot] is zero_in_ref:
            for part in range(2):
                zero_ref[part, slot, pl.ds(PAD, half), :] = zero_in_ref[part, slot, pl.ds(PAD, half), :]

    shards = 2 * send_ref.shape[0]
    shard = lax.axis_index("src")
    shard_rows = size_y // shards
    rows = min(ROWS, shard_rows // 2)
    for slot in range(SWEEPS, SWEEPS + layers):
        layer = layer_of(slot, layers)
        swap = odd_lanes(lax.axis_index("tile") * layers + layer, rows, size_z)
        for m in range(shards):
            ref = send_ref if m % 2 else keep_ref
            start = (shard ^ m) * shard_rows
            for r in range(0, shard_rows // 2, rows):
                at = pl.ds(pl.multiple_of(PAD + start // 2 + r, PAD), rows)
                a = [zero_ref[part, slot, at, :] for part in range(2)]
                b = [one_ref[part, slot, at, :] for part in range(2)]
                for second in range(2):
                    if second:
                        a, b = b, a
                    field = [jnp.where(swap, b[part], a[part]) for part in range(2)]
                    cells = pl.ds(pl.multiple_of(start + 2 * r, 2 * rows) + second, rows, stride=2)
                    products = forward_ref[0, 0, layer, cells, :] * field[1]
                    products += forward_ref[0, 1, layer, cells, :] * field[0]
                    into = pl.ds(2 * r + second, rows, stride=2)
                    ref[m // 2, layer, into, :] = scale_ref[slot - SWEEPS, cells, :] * products


def unpack_kernel(zero_ref, one_ref, out_hbm, out_ref, sems):
    _, layers, size_y, size_z = out_ref.shape
    half = size_y // 2
    rows = min(ROWS, half)
    first = lax.axis_index("tile") * layers
    copies = []
    for slot in range(SWEEPS, SWEEPS + layers):
        layer = layer_of(slot, layers)
        odd = odd_lanes(first + layer, rows, size_z)
        for part in range(2):
            for r in range(0, half, rows):
                a = zero_ref[part, slot, pl.ds(PAD + r, rows), :]
                b = one_ref[part, slot, pl.ds(PAD + r, rows), :]
                out_ref[part, slot - SWEEPS, pl.ds(2 * r, rows, stride=2), :] = jnp.where(odd, b, a)
                out_ref[part, slot - SWEEPS, pl.ds(2 * r + 1, rows, stride=2), :] = jnp.where(odd, a, b)
        i = slot - SWEEPS
        copies.append(
            pltpu.make_async_copy(out_ref.at[:, i], out_hbm.at[0, :, layer], sems.at[i])
        )
        copies[-1].start()
    for copy in copies:
        copy.wait()


def call(kernel, outs, scratch, specs, out_specs, flops, room=20):
    return pl.pallas_call(
        kernel,
        out_shape=[jax.ShapeDtypeStruct(s, jnp.float32) for s in outs],
        in_specs=specs,
        out_specs=out_specs,
        scratch_shapes=scratch,
        compiler_params=pltpu.CompilerParams(vmem_limit_bytes=room << 20),
        cost_estimate=pl.CostEstimate(flops=flops, bytes_accessed=4 << 20, transcendentals=0),
    )


def in_hbm(array):
    return pltpu.with_memory_space_constraint(array, pltpu.HBM)


def floats(*shapes):
    return [pltpu.VMEM(s, jnp.float32) for s in shapes]


def swap_even(count):
    return [(i, i ^ 1) for i in range(count) if i ^ 1 < count]


def swap_odd(count):
    pairs = [(i, i + 1) for i in range(1, count - 1, 2)]
    return pairs + [(b, a) for a, b in pairs]


def body(
    forward_field,
    adjoint_guess,
    conductivity,
    freq_kappa,
    pair_freq,
    recv_data,
    recv_weights,
    recv_x,
    recv_y,
    recv_z,
):
    pairs, _, layers, size_y, size_z = adjoint_guess.shape
    half = size_y // 2
    count, taps = recv_weights.shape
    tiles = lax.axis_size("tile")
    shards = lax.axis_size("src")
    assert pairs == 1 and layers == SWEEPS and count % UNROLL == 0
    cells = len(HALO_CELLS)
    reach = layers + 2 * (SWEEPS - 1)
    slots = layers + 2 * SWEEPS
    evens, odds = swap_even(tiles), swap_odd(tiles)
    flip = [(i, i ^ 1) for i in range(shards)]

    adj, cond_cells = call(
        pack_kernel,
        [(2, layers, half, size_z), (cells, half, size_z)],
        floats((2, layers, size_y, size_z), (layers, size_y, size_z))
        + [pltpu.SemaphoreType.DMA((1 + layers,))],
        [HBM, HBM],
        [VMEM] * 2,
        1 << 20,
        room=20,
    )(in_hbm(adjoint_guess), in_hbm(conductivity))

    mixed = [
        (a * shards + s, b * shards + s)
        for s in range(shards)
        for a, b in (odds if s % 2 else evens)
    ]
    cond_cells = lax.ppermute(cond_cells, ("tile", "src"), mixed)
    adj_odd = lax.ppermute(adj, "tile", odds)
    adj_even = lax.ppermute(adj, "tile", evens)

    source, six_own, cross_own, scale, kappa = call(
        source_kernel,
        [
            (2, 2, reach, half, size_z),
            (2, layers, half, size_z),
            (2, layers, half, size_z),
            (layers, size_y, size_z),
            (8, size_z),
        ],
        [pltpu.SMEM((count,), jnp.int32)] * 3
        + [pltpu.SMEM(freq_kappa.shape, jnp.float32)]
        + floats(
            (taps, count),
            recv_data.shape,
            (layers, size_y, size_z),
            (8 * count, size_z),
            (reach + 8, 2 * size_y, size_z),
        )
        + [pltpu.SemaphoreType.DMA((7,))],
        [HBM] * 4 + [SMEM] + [HBM] * 3,
        [VMEM] * 5,
        1 << 30,
        room=20,
    )(
        in_hbm(recv_x), in_hbm(recv_y), in_hbm(recv_z), in_hbm(freq_kappa), pair_freq,
        in_hbm(recv_weights.T), in_hbm(recv_data), in_hbm(conductivity),
    )

    other_cells = lax.ppermute(cond_cells, "src", flip)

    state = (2, slots, half + 2 * PAD, size_z)
    weights = (2, slots, half, size_z)
    zero, one, six, cross = call(
        near_kernel, [state, state, weights, weights], [], [VMEM] * 8, [VMEM] * 4, 1 << 26
    )(
        adj, adj_even, cond_cells, other_cells, source, six_own, cross_own, kappa
    )

    shard_rows = size_y // shards
    part_shape = (shards // 2, layers, shard_rows, size_z)
    zero, one, send, keep = call(
        far_kernel, [state, state, part_shape, part_shape], [], [VMEM] * 8, [VMEM] * 4, 1 << 26
    )(zero, one, adj_odd, source, six, cross, scale, forward_field)

    (field,) = call(
        unpack_kernel,
        [(1, 2, layers, size_y, size_z)],
        floats((2, layers, size_y, size_z)) + [pltpu.SemaphoreType.DMA((layers,))],
        [VMEM] * 2,
        [HBM],
        1 << 20,
    )(zero, one)

    bit = 1
    while True:
        keep = keep + lax.ppermute(send, "src", [(i, i ^ bit) for i in range(shards)])
        bit *= 2
        if bit == shards:
            break
        send, keep = keep[1::2], keep[0::2]
    return (field, keep[0])


def solution(mesh):
    placed = (
        P(("job", "src"), None, "tile", None, None),
        P(("job", "src"), None, "tile", None, None),
        P(("job", "tile"), None, None),
        P("job"),
        P(("job", "src")),
        P(("job", "src"), None, None),
        P("job", None),
        P("job"),
        P("job"),
        P("job"),
    )
    return jax.shard_map(
        body,
        mesh=mesh,
        in_specs=placed,
        out_specs=(P(("job", "src"), None, "tile", None, None), P(("job", "tile"), "src", None)),
        check_vma=False,
    )
```

```python
import jax
import jax.numpy as jnp
from jax import lax
from jax.experimental import pallas as pl
from jax.experimental.pallas import tpu as pltpu
from jax.sharding import PartitionSpec as P


SWEEPS = 4
COLOURS = tuple(k % 2 for k in range(SWEEPS))
HALO_CELLS = tuple(
    (d, c)
    for d in range(1, SWEEPS)
    for c in (0, 1)
    if any(COLOURS[k] == c and d <= SWEEPS - 1 - k for k in range(SWEEPS))
)
PAD = 8
ROWS = 32
UNROLL = 8
SMEM = pl.BlockSpec(memory_space=pltpu.SMEM)
VMEM = pl.BlockSpec(memory_space=pltpu.VMEM)
HBM = pl.BlockSpec(memory_space=pltpu.HBM)


def odd_lanes(shift, rows, cols):
    return ((lax.broadcasted_iota(jnp.int32, (rows, cols), 1) + shift) & 1) == 1


def of_colour(colour, odd, even_rows, odd_rows):
    if colour == 0:
        return jnp.where(odd, odd_rows, even_rows)
    return jnp.where(odd, even_rows, odd_rows)


def coefficients(kappa, conductivity):
    coupling = kappa * conductivity
    inverse = 1.0 / (36.0 + coupling * coupling)
    return 6.0 * inverse, coupling * inverse


def is_odd(shard):
    return shard % 2 == 1


def is_even(shard):
    return shard % 2 == 0


def near_on_right():
    return (lax.axis_index("tile") % 2 == 0) == is_odd(lax.axis_index("src"))


def layer_of(slot, layers):
    ahead = slot - SWEEPS
    return jnp.where(near_on_right(), layers - 1 - ahead, ahead)


def start_all(copies):
    for copy in copies:
        copy.start()
    return copies


def pack_kernel(guess_hbm, cond_hbm, adj_ref, cells_ref, guess_ref, cond_ref, sems):
    layers, size_y, size_z = cond_ref.shape
    half = size_y // 2
    rows = min(ROWS, half)
    first = lax.axis_index("tile") * layers
    cond_copy = pltpu.make_async_copy(cond_hbm, cond_ref, sems.at[0])
    cond_copy.start()
    guess_copies = start_all(
        [
            pltpu.make_async_copy(guess_hbm.at[0, :, i], guess_ref.at[:, i], sems.at[1 + i])
            for i in range(layers)
        ]
    )
    to_right = jnp.logical_not(near_on_right())
    cond_copy.wait()
    for i, (d, c) in enumerate(HALO_CELLS):
        layer = jnp.where(to_right, layers - d, d - 1)
        odd = odd_lanes(first + layer, rows, size_z)
        for r in range(0, half, rows):
            a = cond_ref[layer, pl.ds(2 * r, rows, stride=2), :]
            b = cond_ref[layer, pl.ds(2 * r + 1, rows, stride=2), :]
            cells_ref[i, pl.ds(r, rows), :] = of_colour(c, odd, a, b)
    for layer in range(layers):
        odd = odd_lanes(first + layer, rows, size_z)
        guess_copies[layer].wait()
        for part in range(2):
            for r in range(0, half, rows):
                a = guess_ref[part, layer, pl.ds(2 * r, rows, stride=2), :]
                b = guess_ref[part, layer, pl.ds(2 * r + 1, rows, stride=2), :]
                adj_ref[part, layer, pl.ds(r, rows), :] = of_colour(1, odd, a, b)


def source_kernel(
    x_hbm, y_hbm, z_hbm, kappas_hbm, freq_ref, weight_hbm, data_hbm, cond_hbm,
    source_ref, six_ref, cross_ref, scale_ref, kappa_ref,
    x_ref, y_ref, z_ref, kappas_ref, weight_ref, data_ref, cond_ref,
    terms_ref, total_ref, sems,
):
    layers, size_y, size_z = cond_ref.shape
    half = size_y // 2
    rows = min(ROWS, half)
    taps, count = weight_ref.shape
    reach = source_ref.shape[2]
    halo = SWEEPS - 1
    first = lax.axis_index("tile") * layers
    copies = start_all(
        [
            pltpu.make_async_copy(a, b, sems.at[i])
            for i, (a, b) in enumerate(
                (
                    (x_hbm, x_ref), (y_hbm, y_ref), (z_hbm, z_ref), (kappas_hbm, kappas_ref),
                    (weight_hbm, weight_ref), (data_hbm, data_ref),
                    (cond_hbm, cond_ref),
                )
            )
        ]
    )
    for layer in range(reach):
        total_ref[4 + layer] = jnp.zeros(total_ref.shape[1:], jnp.float32)
    for copy in copies:
        copy.wait()
    kappa = kappas_ref[freq_ref[0]]
    kappa_ref[...] = jnp.full(kappa_ref.shape, kappa, jnp.float32)

    blank = jnp.zeros((size_z - taps, count), jnp.float32)
    weights = weight_ref[...]
    for c in range(2):
        terms = jnp.concatenate([weights * data_ref[0, c : c + 1, :], blank], axis=0).T
        for b in range(4):
            moved = pltpu.roll(terms, size_z - 4 * b, 1) if b else terms
            terms_ref[pl.ds(2 * b + c, count, stride=8), :] = moved

    lane = lax.broadcasted_iota(jnp.int32, (8, size_z), 1)

    def add_block(r):
        z = z_ref[r]
        base = jnp.clip(x_ref[r] - first + halo, -4, reach) + 4
        row = 2 * y_ref[r]
        inside = (lane - z).astype(jnp.uint32) < 4
        both = terms_ref[pl.ds(pl.multiple_of(8 * r, 8), 8), :]
        terms = []
        for a in range(4):
            moved = pltpu.roll(both, lax.rem(z + size_z - 16 * a, size_z), 1)
            terms.append(jnp.where(inside, moved, 0.0))
        old = [total_ref[base + a, pl.ds(row, 8), :] for a in range(4)]
        for a in range(4):
            total_ref[base + a, pl.ds(row, 8), :] = old[a] + terms[a]

    def some_blocks(step, carry):
        for u in range(UNROLL):
            add_block(step * UNROLL + u)
        return carry

    lax.fori_loop(0, count // UNROLL, some_blocks, 0)

    for ahead in range(layers):
        layer = layer_of(SWEEPS + ahead, layers)
        odd = odd_lanes(first + layer, rows, size_z)
        for r in range(0, half, rows):
            a = cond_ref[layer, pl.ds(2 * r, rows, stride=2), :]
            b = cond_ref[layer, pl.ds(2 * r + 1, rows, stride=2), :]
            for c in (0, 1):
                six, cross = coefficients(kappa, of_colour(c, odd, a, b))
                six_ref[c, ahead, pl.ds(r, rows), :] = six
                cross_ref[c, ahead, pl.ds(r, rows), :] = cross
        scale_ref[ahead] = -(kappa * cond_ref[layer])

    def pack_layer(i, carry):
        layer = layer_of(i + 1, layers)
        odd = odd_lanes(first + layer, rows, size_z)
        for part in range(2):
            for r in range(0, half, rows):
                a = total_ref[4 + halo + layer, pl.ds(4 * r + part, rows, stride=4), :]
                b = total_ref[4 + halo + layer, pl.ds(4 * r + 2 + part, rows, stride=4), :]
                for c in (0, 1):
                    source_ref[c, part, i, pl.ds(r, rows), :] = of_colour(c, odd, a, b)
        return carry

    lax.fori_loop(0, reach, pack_layer, 0)


class Sweeper:
    def __init__(self, half, size_z, layers, source, six, cross):
        self.half, self.size_z = half, size_z
        self.source, self.six, self.cross = source, six, cross
        self.where = ({}, {})
        first = lax.axis_index("tile") * layers
        self.rows = min(ROWS, half)
        base = first + jnp.where(near_on_right(), layers - 1, 0)
        self.odd = odd_lanes(base, self.rows, size_z)
        lane = lax.broadcasted_iota(jnp.int32, (self.rows, size_z), 1)
        self.after, self.before = lane > 0, lane < size_z - 1
        near = lax.broadcasted_iota(jnp.int32, (size_z, size_z), 0)
        near = jnp.abs(near - lax.broadcasted_iota(jnp.int32, (size_z, size_z), 1)) <= 1
        near = jnp.where(near, 1.0, 0.0).astype(jnp.bfloat16)
        self.near = jnp.concatenate([near] * 3, axis=0)

    def along_z(self, values):
        high = values.astype(jnp.bfloat16)
        rest = values - high.astype(jnp.float32)
        middle = rest.astype(jnp.bfloat16)
        low = (rest - middle.astype(jnp.float32)).astype(jnp.bfloat16)
        pieces = jnp.concatenate([high, middle, low], axis=1)
        return jnp.dot(pieces, self.near, preferred_element_type=jnp.float32)

    def sums(self, c, part, slot):
        old = self.where[1 - c]
        here, left, right = old[slot], old[slot - 1], old[slot + 1]
        rows = self.rows
        by_matrix = part == 1
        if by_matrix:
            beside = self.along_z(here[part, slot, pl.ds(PAD, self.half), :])
        out = []
        for r in range(0, self.half, rows):
            above = here[part, slot, pl.ds(PAD + r + 1, rows), :]
            below = here[part, slot, pl.ds(PAD + r - 1, rows), :]
            if (slot + c) % 2:
                above, below = below, above
            total = left[part, slot - 1, pl.ds(PAD + r, rows), :]
            total += right[part, slot + 1, pl.ds(PAD + r, rows), :]
            total += jnp.where(self.odd, above, below)
            if by_matrix:
                total += beside[r : r + rows]
            else:
                centre = here[part, slot, pl.ds(PAD + r, rows), :]
                total += centre
                total += jnp.where(self.after, pltpu.roll(centre, 1, 1), 0.0)
                total += jnp.where(self.before, pltpu.roll(centre, self.size_z - 1, 1), 0.0)
            out.append(total + self.source[c, part, slot - 1, pl.ds(r, rows), :])
        return out

    def update(self, c, slot, new):
        sums = [self.sums(c, part, slot) for part in range(2)]
        for i, r in enumerate(range(0, self.half, self.rows)):
            six = self.six[c, slot, pl.ds(r, self.rows), :]
            cross = self.cross[c, slot, pl.ds(r, self.rows), :]
            at = pl.ds(PAD + r, self.rows)
            new[0, slot, at, :] = six * sums[0][i] + cross * sums[1][i]
            new[1, slot, at, :] = six * sums[1][i] - cross * sums[0][i]
        self.where[c][slot] = new


def clear_edges(ref, slots, half):
    edge = jnp.zeros((PAD, ref.shape[-1]), jnp.float32)
    for part in range(2):
        for slot in slots:
            ref[part, slot, pl.ds(0, PAD), :] = edge
            ref[part, slot, pl.ds(PAD + half, PAD), :] = edge


def near_kernel(
    adj_ref, halo_ref, far_cells_ref, near_cells_ref,
    source_ref, six_own_ref, cross_own_ref, kappa_ref,
    zero_ref, one_ref, six_ref, cross_ref,
):
    _, layers, half, size_z = adj_ref.shape
    tile, tiles = lax.axis_index("tile"), lax.axis_size("tile")
    on_right = near_on_right()
    rows = min(ROWS, half)
    reached = layers + SWEEPS
    is_last, is_first = tile == tiles - 1, tile == 0
    clear_edges(zero_ref, range(1, reached - 1), half)
    clear_edges(one_ref, range(reached), half)
    for part in range(2):
        for slot in range(reached):
            layer = layer_of(slot, layers)
            if slot < SWEEPS:
                values = halo_ref[part, jnp.where(on_right, layer - layers, layer + SWEEPS)]
                values = jnp.where(jnp.where(on_right, is_last, is_first), 0.0, values)
            else:
                values = adj_ref[part, layer]
            one_ref[part, slot, pl.ds(PAD, half), :] = values
    for c in (0, 1):
        for layer in range(layers):
            six_ref[c, SWEEPS + layer] = six_own_ref[c, layer]
            cross_ref[c, SWEEPS + layer] = cross_own_ref[c, layer]
    kappa = jnp.broadcast_to(kappa_ref[0:1, :], (rows, size_z))
    for ref, is_near in ((near_cells_ref, True), (far_cells_ref, False)):
        missing = jnp.where(on_right, is_last, is_first)
        if not is_near:
            missing = jnp.where(on_right, is_first, is_last)
        there = jnp.where(missing, 0.0, 1.0)
        for i, (d, c) in enumerate(HALO_CELLS):
            slot = SWEEPS - d if is_near else SWEEPS + layers - 1 + d
            for r in range(0, half, rows):
                six, cross = coefficients(kappa, ref[i, pl.ds(r, rows), :])
                six_ref[c, slot, pl.ds(r, rows), :] = six * there
                cross_ref[c, slot, pl.ds(r, rows), :] = cross * there
    sweeper = Sweeper(half, size_z, layers, source_ref, six_ref, cross_ref)
    sweeper.where[1].update({slot: one_ref for slot in range(reached)})
    for k, c in enumerate(COLOURS):
        for slot in range(1 + k, reached - 1 - k):
            sweeper.update(c, slot, (zero_ref, one_ref)[c])


def far_kernel(
    zero_in_ref, one_in_ref, halo_ref, source_ref, six_ref, cross_ref, scale_ref, forward_ref,
    zero_ref, one_ref, send_ref, keep_ref,
):
    _, slots, _, size_z = zero_in_ref.shape
    layers, size_y, _ = scale_ref.shape
    half = size_y // 2
    tile, tiles = lax.axis_index("tile"), lax.axis_size("tile")
    on_right = near_on_right()
    reached = layers + SWEEPS
    clear_edges(zero_ref, range(SWEEPS, slots - 1), half)
    clear_edges(one_ref, range(SWEEPS, slots), half)
    for part in range(2):
        for slot in range(reached, slots):
            layer = layer_of(slot, layers)
            values = halo_ref[part, jnp.where(on_right, layer + SWEEPS, layer - layers)]
            values = jnp.where(jnp.where(on_right, tile == 0, tile == tiles - 1), 0.0, values)
            one_ref[part, slot, pl.ds(PAD, half), :] = values
    sweeper = Sweeper(half, size_z, layers, source_ref, six_ref, cross_ref)
    sweeper.where[0].update({slot: zero_in_ref for slot in range(1, reached - 1)})
    sweeper.where[1].update({slot: one_in_ref for slot in range(reached)})
    sweeper.where[1].update({slot: one_ref for slot in range(reached, slots)})
    for k, c in enumerate(COLOURS):
        for slot in range(reached - 1 - k, slots - 1 - k):
            sweeper.update(c, slot, (zero_ref, one_ref)[c])
    for slot in range(SWEEPS, SWEEPS + layers):
        if sweeper.where[0][slot] is zero_in_ref:
            for part in range(2):
                zero_ref[part, slot, pl.ds(PAD, half), :] = zero_in_ref[part, slot, pl.ds(PAD, half), :]

    shards = 2 * send_ref.shape[0]
    shard = lax.axis_index("src")
    shard_rows = size_y // shards
    rows = min(ROWS, shard_rows // 2)
    for slot in range(SWEEPS, SWEEPS + layers):
        layer = layer_of(slot, layers)
        swap = odd_lanes(lax.axis_index("tile") * layers + layer, rows, size_z)
        for m in range(shards):
            ref = send_ref if m % 2 else keep_ref
            start = (shard ^ m) * shard_rows
            for r in range(0, shard_rows // 2, rows):
                at = pl.ds(pl.multiple_of(PAD + start // 2 + r, PAD), rows)
                a = [zero_ref[part, slot, at, :] for part in range(2)]
                b = [one_ref[part, slot, at, :] for part in range(2)]
                for second in range(2):
                    if second:
                        a, b = b, a
                    field = [jnp.where(swap, b[part], a[part]) for part in range(2)]
                    cells = pl.ds(pl.multiple_of(start + 2 * r, 2 * rows) + second, rows, stride=2)
                    products = forward_ref[0, 0, layer, cells, :] * field[1]
                    products += forward_ref[0, 1, layer, cells, :] * field[0]
                    into = pl.ds(2 * r + second, rows, stride=2)
                    ref[m // 2, layer, into, :] = scale_ref[slot - SWEEPS, cells, :] * products


def unpack_kernel(zero_ref, one_ref, out_hbm, out_ref, sems):
    _, layers, size_y, size_z = out_ref.shape
    half = size_y // 2
    rows = min(ROWS, half)
    first = lax.axis_index("tile") * layers
    copies = []
    for slot in range(SWEEPS, SWEEPS + layers):
        layer = layer_of(slot, layers)
        odd = odd_lanes(first + layer, rows, size_z)
        for part in range(2):
            for r in range(0, half, rows):
                a = zero_ref[part, slot, pl.ds(PAD + r, rows), :]
                b = one_ref[part, slot, pl.ds(PAD + r, rows), :]
                out_ref[part, slot - SWEEPS, pl.ds(2 * r, rows, stride=2), :] = jnp.where(odd, b, a)
                out_ref[part, slot - SWEEPS, pl.ds(2 * r + 1, rows, stride=2), :] = jnp.where(odd, a, b)
        i = slot - SWEEPS
        copies.append(
            pltpu.make_async_copy(out_ref.at[:, i], out_hbm.at[0, :, layer], sems.at[i])
        )
        copies[-1].start()
    for copy in copies:
        copy.wait()


def call(kernel, outs, scratch, specs, out_specs, flops, room=20):
    return pl.pallas_call(
        kernel,
        out_shape=[jax.ShapeDtypeStruct(s, jnp.float32) for s in outs],
        in_specs=specs,
        out_specs=out_specs,
        scratch_shapes=scratch,
        compiler_params=pltpu.CompilerParams(vmem_limit_bytes=room << 20),
        cost_estimate=pl.CostEstimate(flops=flops, bytes_accessed=4 << 20, transcendentals=0),
    )


def in_hbm(array):
    return pltpu.with_memory_space_constraint(array, pltpu.HBM)


def floats(*shapes):
    return [pltpu.VMEM(s, jnp.float32) for s in shapes]


def swaps(tiles, shards, odd_of):
    pairs = []
    for t in range(tiles):
        for s in range(shards):
            other = (t + 1 ^ 1) - 1 if odd_of(s) else t ^ 1
            to = (other, s) if 0 <= other < tiles else (t, spare(s, shards, odd_of))
            pairs.append((t * shards + s, to[0] * shards + to[1]))
    return pairs


def spare(s, shards, odd_of):
    return next((o for o in (s ^ 1, s ^ 2) if o < shards and odd_of(o) == odd_of(s)), s)


def body(
    forward_field,
    adjoint_guess,
    conductivity,
    freq_kappa,
    pair_freq,
    recv_data,
    recv_weights,
    recv_x,
    recv_y,
    recv_z,
):
    pairs, _, layers, size_y, size_z = adjoint_guess.shape
    half = size_y // 2
    count, taps = recv_weights.shape
    tiles = lax.axis_size("tile")
    shards = lax.axis_size("src")
    assert pairs == 1 and layers == SWEEPS and count % UNROLL == 0
    cells = len(HALO_CELLS)
    reach = layers + 2 * (SWEEPS - 1)
    slots = layers + 2 * SWEEPS
    flip = [(i, i ^ 1) for i in range(shards)]

    adj, cells_out = call(
        pack_kernel,
        [(2, layers, half, size_z), (cells, half, size_z)],
        floats((2, layers, size_y, size_z), (layers, size_y, size_z))
        + [pltpu.SemaphoreType.DMA((1 + layers,))],
        [HBM, HBM],
        [VMEM] * 2,
        1 << 20,
        room=20,
    )(in_hbm(adjoint_guess), in_hbm(conductivity))

    both = ("tile", "src")
    to_near = swaps(tiles, shards, is_even)
    to_far = swaps(tiles, shards, is_odd)
    far_cells = lax.ppermute(cells_out, both, to_far)
    near_halo = lax.ppermute(adj, both, to_near)
    far_halo = lax.ppermute(adj, both, to_far)

    source, six_own, cross_own, scale, kappa = call(
        source_kernel,
        [
            (2, 2, reach, half, size_z),
            (2, layers, half, size_z),
            (2, layers, half, size_z),
            (layers, size_y, size_z),
            (8, size_z),
        ],
        [pltpu.SMEM((count,), jnp.int32)] * 3
        + [pltpu.SMEM(freq_kappa.shape, jnp.float32)]
        + floats(
            (taps, count),
            recv_data.shape,
            (layers, size_y, size_z),
            (8 * count, size_z),
            (reach + 8, 2 * size_y, size_z),
        )
        + [pltpu.SemaphoreType.DMA((7,))],
        [HBM] * 4 + [SMEM] + [HBM] * 3,
        [VMEM] * 5,
        1 << 30,
        room=20,
    )(
        in_hbm(recv_x), in_hbm(recv_y), in_hbm(recv_z), in_hbm(freq_kappa), pair_freq,
        in_hbm(recv_weights.T), in_hbm(recv_data), in_hbm(conductivity),
    )

    near_cells = lax.ppermute(far_cells, "src", flip)

    state = (2, slots, half + 2 * PAD, size_z)
    weights = (2, slots, half, size_z)
    zero, one, six, cross = call(
        near_kernel, [state, state, weights, weights], [], [VMEM] * 8, [VMEM] * 4, 1 << 26
    )(
        adj, near_halo, far_cells, near_cells, source, six_own, cross_own, kappa
    )

    shard_rows = size_y // shards
    part_shape = (shards // 2, layers, shard_rows, size_z)
    zero, one, send, keep = call(
        far_kernel, [state, state, part_shape, part_shape], [], [VMEM] * 8, [VMEM] * 4, 1 << 26
    )(zero, one, far_halo, source, six, cross, scale, forward_field)

    (field,) = call(
        unpack_kernel,
        [(1, 2, layers, size_y, size_z)],
        floats((2, layers, size_y, size_z)) + [pltpu.SemaphoreType.DMA((layers,))],
        [VMEM] * 2,
        [HBM],
        1 << 20,
    )(zero, one)

    bit = 1
    while True:
        keep = keep + lax.ppermute(send, "src", [(i, i ^ bit) for i in range(shards)])
        bit *= 2
        if bit == shards:
            break
        send, keep = keep[1::2], keep[0::2]
    return (field, keep[0])


def solution(mesh):
    placed = (
        P(("job", "src"), None, "tile", None, None),
        P(("job", "src"), None, "tile", None, None),
        P(("job", "tile"), None, None),
        P("job"),
        P(("job", "src")),
        P(("job", "src"), None, None),
        P("job", None),
        P("job"),
        P("job"),
        P("job"),
    )
    return jax.shard_map(
        body,
        mesh=mesh,
        in_specs=placed,
        out_specs=(P(("job", "src"), None, "tile", None, None), P(("job", "tile"), "src", None)),
        check_vma=False,
    )
```

```python
import jax
import jax.numpy as jnp
from jax import lax
from jax.experimental import pallas as pl
from jax.experimental.pallas import tpu as pltpu
from jax.sharding import PartitionSpec as P


SWEEPS = 4
COLOURS = tuple(k % 2 for k in range(SWEEPS))
HALO_CELLS = tuple(
    (d, c)
    for d in range(1, SWEEPS)
    for c in (0, 1)
    if any(COLOURS[k] == c and d <= SWEEPS - 1 - k for k in range(SWEEPS))
)
PAD = 8
ROWS = 32
UNROLL = 32
SMEM = pl.BlockSpec(memory_space=pltpu.SMEM)
VMEM = pl.BlockSpec(memory_space=pltpu.VMEM)
HBM = pl.BlockSpec(memory_space=pltpu.HBM)


def odd_lanes(shift, rows, cols):
    return ((lax.broadcasted_iota(jnp.int32, (rows, cols), 1) + shift) & 1) == 1


def of_colour(colour, odd, even_rows, odd_rows):
    if colour == 0:
        return jnp.where(odd, odd_rows, even_rows)
    return jnp.where(odd, even_rows, odd_rows)


def coefficients(kappa, conductivity):
    coupling = kappa * conductivity
    inverse = 1.0 / (36.0 + coupling * coupling)
    return 6.0 * inverse, coupling * inverse


def is_odd(shard):
    return shard % 2 == 1


def is_even(shard):
    return shard % 2 == 0


def near_on_right():
    return (lax.axis_index("tile") % 2 == 0) == is_odd(lax.axis_index("src"))


def layer_of(slot, layers):
    ahead = slot - SWEEPS
    return jnp.where(near_on_right(), layers - 1 - ahead, ahead)


def start_all(copies):
    for copy in copies:
        copy.start()
    return copies


def pack_kernel(guess_hbm, adj_ref, first_ref, second_ref, guess_ref, sems):
    _, layers, half, size_z = adj_ref.shape
    rows = min(ROWS, half)
    first = lax.axis_index("tile") * layers
    depth = first_ref.shape[1]
    copies = start_all(
        [
            pltpu.make_async_copy(guess_hbm.at[0, :, i], guess_ref.at[:, i], sems.at[i])
            for i in range(layers)
        ]
    )
    for layer in range(layers):
        odd = odd_lanes(first + layer, rows, size_z)
        copies[layer].wait()
        for part in range(2):
            for r in range(0, half, rows):
                a = guess_ref[part, layer, pl.ds(2 * r, rows, stride=2), :]
                b = guess_ref[part, layer, pl.ds(2 * r + 1, rows, stride=2), :]
                adj_ref[part, layer, pl.ds(r, rows), :] = of_colour(1, odd, a, b)
    for d in range(SWEEPS):
        layer = layer_of(SWEEPS + layers - 1 - d, layers)
        ref = (first_ref, second_ref)[d // depth]
        for part in range(2):
            ref[part, d % depth] = adj_ref[part, layer]


def cells_kernel(cond_hbm, cells_ref, cond_ref, sems):
    layers = cond_hbm.shape[0]
    deep, size_y, size_z = cond_ref.shape
    half = size_y // 2
    rows = min(ROWS, half)
    to_right = jnp.logical_not(near_on_right())
    base = jnp.where(to_right, layers - deep, 0)
    copy = pltpu.make_async_copy(cond_hbm.at[pl.ds(base, deep)], cond_ref, sems.at[0])
    copy.start()
    copy.wait()
    first = lax.axis_index("tile") * layers + base
    for i, (d, c) in enumerate(HALO_CELLS):
        layer = jnp.where(to_right, deep - d, d - 1)
        odd = odd_lanes(first + layer, rows, size_z)
        for r in range(0, half, rows):
            a = cond_ref[layer, pl.ds(2 * r, rows, stride=2), :]
            b = cond_ref[layer, pl.ds(2 * r + 1, rows, stride=2), :]
            cells_ref[i, pl.ds(r, rows), :] = of_colour(c, odd, a, b)


def source_kernel(
    x_hbm, y_hbm, z_hbm, kappas_hbm, freq_ref, weight_hbm, data_hbm, cond_hbm,
    source_ref, six_ref, cross_ref, scale_ref, kappa_ref,
    x_ref, y_ref, z_ref, kappas_ref, weight_ref, data_ref, cond_ref,
    terms_ref, total_ref, sems,
):
    layers, size_y, size_z = cond_ref.shape
    half = size_y // 2
    rows = min(ROWS, half)
    taps, count = weight_ref.shape
    reach = source_ref.shape[2]
    halo = SWEEPS - 1
    first = lax.axis_index("tile") * layers
    copies = start_all(
        [
            pltpu.make_async_copy(a, b, sems.at[i])
            for i, (a, b) in enumerate(
                (
                    (x_hbm, x_ref), (y_hbm, y_ref), (z_hbm, z_ref), (kappas_hbm, kappas_ref),
                    (weight_hbm, weight_ref), (data_hbm, data_ref),
                    (cond_hbm, cond_ref),
                )
            )
        ]
    )
    for layer in range(reach):
        total_ref[4 + layer] = jnp.zeros(total_ref.shape[1:], jnp.float32)
    for copy in copies:
        copy.wait()
    kappa = kappas_ref[freq_ref[0]]
    kappa_ref[...] = jnp.full(kappa_ref.shape, kappa, jnp.float32)

    blank = jnp.zeros((size_z - taps, count), jnp.float32)
    weights = weight_ref[...]
    for c in range(2):
        terms = jnp.concatenate([weights * data_ref[0, c : c + 1, :], blank], axis=0).T
        for b in range(4):
            moved = pltpu.roll(terms, size_z - 4 * b, 1) if b else terms
            terms_ref[pl.ds(2 * b + c, count, stride=8), :] = moved

    lane = lax.broadcasted_iota(jnp.int32, (8, size_z), 1)

    def add_block(r):
        z = z_ref[r]
        base = jnp.clip(x_ref[r] - first + halo, -4, reach) + 4
        row = 2 * y_ref[r]
        inside = (lane - z).astype(jnp.uint32) < 4
        first_tap = pltpu.roll(terms_ref[pl.ds(pl.multiple_of(8 * r, 8), 8), :], z, 1)
        terms = []
        for a in range(4):
            moved = pltpu.roll(first_tap, size_z - 16 * a, 1) if a else first_tap
            terms.append(jnp.where(inside, moved, 0.0))
        old = [total_ref[base + a, pl.ds(row, 8), :] for a in range(4)]
        for a in range(4):
            total_ref[base + a, pl.ds(row, 8), :] = old[a] + terms[a]

    def some_blocks(step, carry):
        for u in range(UNROLL):
            add_block(step * UNROLL + u)
        return carry

    lax.fori_loop(0, count // UNROLL, some_blocks, 0)

    for ahead in range(layers):
        layer = layer_of(SWEEPS + ahead, layers)
        odd = odd_lanes(first + layer, rows, size_z)
        for r in range(0, half, rows):
            a = cond_ref[layer, pl.ds(2 * r, rows, stride=2), :]
            b = cond_ref[layer, pl.ds(2 * r + 1, rows, stride=2), :]
            for c in (0, 1):
                six, cross = coefficients(kappa, of_colour(c, odd, a, b))
                six_ref[c, ahead, pl.ds(r, rows), :] = six
                cross_ref[c, ahead, pl.ds(r, rows), :] = cross
        scale_ref[ahead] = -(kappa * cond_ref[layer])

    def pack_layer(i, carry):
        layer = layer_of(i + 1, layers)
        odd = odd_lanes(first + layer, rows, size_z)
        for part in range(2):
            for r in range(0, half, rows):
                a = total_ref[4 + halo + layer, pl.ds(4 * r + part, rows, stride=4), :]
                b = total_ref[4 + halo + layer, pl.ds(4 * r + 2 + part, rows, stride=4), :]
                for c in (0, 1):
                    source_ref[c, part, i, pl.ds(r, rows), :] = of_colour(c, odd, a, b)
        return carry

    lax.fori_loop(0, reach, pack_layer, 0)


class Sweeper:
    def __init__(self, half, size_z, layers, source, six, cross):
        self.half, self.size_z = half, size_z
        self.source, self.six, self.cross = source, six, cross
        self.where = ({}, {})
        first = lax.axis_index("tile") * layers
        self.rows = min(ROWS, half)
        base = first + jnp.where(near_on_right(), layers - 1, 0)
        self.odd = odd_lanes(base, self.rows, size_z)
        lane = lax.broadcasted_iota(jnp.int32, (self.rows, size_z), 1)
        self.after, self.before = lane > 0, lane < size_z - 1
        near = lax.broadcasted_iota(jnp.int32, (size_z, size_z), 0)
        near = jnp.abs(near - lax.broadcasted_iota(jnp.int32, (size_z, size_z), 1)) <= 1
        near = jnp.where(near, 1.0, 0.0).astype(jnp.bfloat16)
        self.near = jnp.concatenate([near] * 3, axis=0)

    def along_z(self, values):
        high = values.astype(jnp.bfloat16)
        rest = values - high.astype(jnp.float32)
        middle = rest.astype(jnp.bfloat16)
        low = (rest - middle.astype(jnp.float32)).astype(jnp.bfloat16)
        pieces = jnp.concatenate([high, middle, low], axis=1)
        return jnp.dot(pieces, self.near, preferred_element_type=jnp.float32)

    def sums(self, c, part, slot):
        old = self.where[1 - c]
        (here, at_here), (left, at_left), (right, at_right) = old[slot], old[slot - 1], old[slot + 1]
        rows = self.rows
        by_matrix = part == 1
        if by_matrix:
            beside = self.along_z(here[part, at_here, pl.ds(PAD, self.half), :])
        out = []
        for r in range(0, self.half, rows):
            above = here[part, at_here, pl.ds(PAD + r + 1, rows), :]
            below = here[part, at_here, pl.ds(PAD + r - 1, rows), :]
            if (slot + c) % 2:
                above, below = below, above
            total = left[part, at_left, pl.ds(PAD + r, rows), :]
            total += right[part, at_right, pl.ds(PAD + r, rows), :]
            total += jnp.where(self.odd, above, below)
            if by_matrix:
                total += beside[r : r + rows]
            else:
                centre = here[part, at_here, pl.ds(PAD + r, rows), :]
                total += centre
                total += jnp.where(self.after, pltpu.roll(centre, 1, 1), 0.0)
                total += jnp.where(self.before, pltpu.roll(centre, self.size_z - 1, 1), 0.0)
            out.append(total + self.source[c, part, slot - 1, pl.ds(r, rows), :])
        return out

    def update(self, c, slot, new, index):
        sums = [self.sums(c, part, slot) for part in range(2)]
        for i, r in enumerate(range(0, self.half, self.rows)):
            six = self.six[c, slot, pl.ds(r, self.rows), :]
            cross = self.cross[c, slot, pl.ds(r, self.rows), :]
            at = pl.ds(PAD + r, self.rows)
            new[0, index, at, :] = six * sums[0][i] + cross * sums[1][i]
            new[1, index, at, :] = six * sums[1][i] - cross * sums[0][i]
        self.where[c][slot] = (new, index)


def clear_edges(ref, slots, half):
    edge = jnp.zeros((PAD, ref.shape[-1]), jnp.float32)
    for part in range(2):
        for slot in slots:
            ref[part, slot, pl.ds(0, PAD), :] = edge
            ref[part, slot, pl.ds(PAD + half, PAD), :] = edge


def near_kernel(
    adj_ref, halo_ref, far_cells_ref, near_cells_ref,
    source_ref, six_own_ref, cross_own_ref, kappa_ref,
    zero_ref, one_ref, six_ref, cross_ref,
):
    _, layers, half, size_z = adj_ref.shape
    tile, tiles = lax.axis_index("tile"), lax.axis_size("tile")
    on_right = near_on_right()
    rows = min(ROWS, half)
    reached = layers + SWEEPS
    is_last, is_first = tile == tiles - 1, tile == 0
    clear_edges(zero_ref, range(1, reached - 1), half)
    clear_edges(one_ref, range(reached), half)
    for part in range(2):
        for slot in range(reached):
            layer = layer_of(slot, layers)
            if slot < SWEEPS:
                values = halo_ref[part, jnp.where(on_right, layer - layers, layer + SWEEPS)]
                values = jnp.where(jnp.where(on_right, is_last, is_first), 0.0, values)
            else:
                values = adj_ref[part, layer]
            one_ref[part, slot, pl.ds(PAD, half), :] = values
    for c in (0, 1):
        for layer in range(layers):
            six_ref[c, SWEEPS + layer] = six_own_ref[c, layer]
            cross_ref[c, SWEEPS + layer] = cross_own_ref[c, layer]
    kappa = jnp.broadcast_to(kappa_ref[0:1, :], (rows, size_z))
    for ref, is_near in ((near_cells_ref, True), (far_cells_ref, False)):
        missing = jnp.where(on_right, is_last, is_first)
        if not is_near:
            missing = jnp.where(on_right, is_first, is_last)
        there = jnp.where(missing, 0.0, 1.0)
        for i, (d, c) in enumerate(HALO_CELLS):
            slot = SWEEPS - d if is_near else SWEEPS + layers - 1 + d
            for r in range(0, half, rows):
                six, cross = coefficients(kappa, ref[i, pl.ds(r, rows), :])
                six_ref[c, slot, pl.ds(r, rows), :] = six * there
                cross_ref[c, slot, pl.ds(r, rows), :] = cross * there
    sweeper = Sweeper(half, size_z, layers, source_ref, six_ref, cross_ref)
    sweeper.where[1].update({slot: (one_ref, slot) for slot in range(reached)})
    for k, c in enumerate(COLOURS):
        for slot in range(1 + k, reached - 1 - k):
            sweeper.update(c, slot, (zero_ref, one_ref)[c], slot)


def gradient_terms(slots, zeros, ones, scale_ref, forward_ref, send_ref, keep_ref):
    layers, size_y, size_z = scale_ref.shape
    shards = 2 * send_ref.shape[0]
    shard = lax.axis_index("src")
    shard_rows = size_y // shards
    rows = min(ROWS, shard_rows // 2)
    for slot in slots:
        layer = layer_of(slot, layers)
        swap = odd_lanes(lax.axis_index("tile") * layers + layer, rows, size_z)
        for m in range(shards):
            ref = send_ref if m % 2 else keep_ref
            start = (shard ^ m) * shard_rows
            for r in range(0, shard_rows // 2, rows):
                at = pl.ds(pl.multiple_of(PAD + start // 2 + r, PAD), rows)
                a, b = (
                    [ref[part, i, at, :] for part in range(2)]
                    for ref, i in (zeros[slot], ones[slot])
                )
                for second in range(2):
                    if second:
                        a, b = b, a
                    field = [jnp.where(swap, b[part], a[part]) for part in range(2)]
                    cells = pl.ds(pl.multiple_of(start + 2 * r, 2 * rows) + second, rows, stride=2)
                    products = forward_ref[0, 0, layer, cells, :] * field[1]
                    products += forward_ref[0, 1, layer, cells, :] * field[0]
                    into = pl.ds(2 * r + second, rows, stride=2)
                    ref[m // 2, layer % len(slots), into, :] = (
                        scale_ref[slot - SWEEPS, cells, :] * products
                    )


def far_sweeps(begin, depth, halo_ref, source_ref, six_ref, cross_ref, scale_ref, older, zero_ref, one_ref):
    layers, size_y, size_z = scale_ref.shape
    half = size_y // 2
    tile, tiles = lax.axis_index("tile"), lax.axis_size("tile")
    missing = jnp.where(near_on_right(), tile == 0, tile == tiles - 1)
    bases = (begin - SWEEPS + 1, begin - SWEEPS)
    clear_edges(zero_ref, range(zero_ref.shape[1]), half)
    clear_edges(one_ref, range(one_ref.shape[1]), half)
    for part in range(2):
        for d in range(depth):
            values = jnp.where(missing, 0.0, halo_ref[part, d])
            one_ref[part, begin + d - bases[1], pl.ds(PAD, half), :] = values
    sweeper = Sweeper(half, size_z, layers, source_ref, six_ref, cross_ref)
    for c in (0, 1):
        sweeper.where[c].update(older[c])
    sweeper.where[1].update({begin + d: (one_ref, begin + d - bases[1]) for d in range(depth)})
    for k, c in enumerate(COLOURS):
        for slot in range(begin - 1 - k, begin + depth - 1 - k):
            sweeper.update(c, slot, (zero_ref, one_ref)[c], slot - bases[c])
    return sweeper.where


def near_values(zero_ref, one_ref):
    reached = 2 * SWEEPS
    return (
        {slot: (zero_ref, slot) for slot in range(1, reached - 1)},
        {slot: (one_ref, slot) for slot in range(reached)},
    )


def first_kernel(
    zero_in_ref, one_in_ref, halo_ref, source_ref, six_ref, cross_ref, scale_ref, forward_ref,
    zero_ref, one_ref, send_ref, keep_ref,
):
    depth = halo_ref.shape[1]
    zeros, ones = far_sweeps(
        2 * SWEEPS, depth, halo_ref, source_ref, six_ref, cross_ref, scale_ref,
        near_values(zero_in_ref, one_in_ref), zero_ref, one_ref,
    )
    done = range(SWEEPS, SWEEPS + depth)
    gradient_terms(done, zeros, ones, scale_ref, forward_ref, send_ref, keep_ref)


def second_kernel(
    zero_in_ref, one_in_ref, halo_ref, source_ref, six_ref, cross_ref, scale_ref, forward_ref,
    zero_ref, one_ref, send_ref, keep_ref,
):
    depth = halo_ref.shape[1]
    begin = 2 * SWEEPS + depth
    older = (
        {SWEEPS + 1 + i: (zero_in_ref, i) for i in range(zero_in_ref.shape[1])},
        {SWEEPS + i: (one_in_ref, i) for i in range(one_in_ref.shape[1])},
    )
    zeros, ones = far_sweeps(
        begin, depth, halo_ref, source_ref, six_ref, cross_ref, scale_ref, older, zero_ref, one_ref
    )
    done = range(SWEEPS + depth, SWEEPS + 2 * depth)
    gradient_terms(done, zeros, ones, scale_ref, forward_ref, send_ref, keep_ref)


def unpack_kernel(near_ref, zero_a_ref, one_a_ref, zero_b_ref, one_b_ref, out_hbm, out_ref, sems):
    _, layers, size_y, size_z = out_ref.shape
    depth = layers // 2
    zeros = [(near_ref, SWEEPS)] + [(zero_a_ref, i) for i in range(depth)]
    zeros += [(zero_b_ref, i) for i in range(depth - 1)]
    ones = [(ref, i) for ref in (one_a_ref, one_b_ref) for i in range(depth)]
    half = size_y // 2
    rows = min(ROWS, half)
    first = lax.axis_index("tile") * layers
    copies = []
    for slot in range(SWEEPS, SWEEPS + layers):
        layer = layer_of(slot, layers)
        odd = odd_lanes(first + layer, rows, size_z)
        for part in range(2):
            for r in range(0, half, rows):
                a = zeros[slot - SWEEPS][0][part, zeros[slot - SWEEPS][1], pl.ds(PAD + r, rows), :]
                b = ones[slot - SWEEPS][0][part, ones[slot - SWEEPS][1], pl.ds(PAD + r, rows), :]
                out_ref[part, slot - SWEEPS, pl.ds(2 * r, rows, stride=2), :] = jnp.where(odd, b, a)
                out_ref[part, slot - SWEEPS, pl.ds(2 * r + 1, rows, stride=2), :] = jnp.where(odd, a, b)
        i = slot - SWEEPS
        copies.append(
            pltpu.make_async_copy(out_ref.at[:, i], out_hbm.at[0, :, layer], sems.at[i])
        )
        copies[-1].start()
    for copy in copies:
        copy.wait()


def join_kernel(keep_a_ref, got_a_ref, keep_b_ref, got_b_ref, send_ref, keep_ref):
    depth = keep_a_ref.shape[1]
    begun = jnp.where(near_on_right(), depth, 0)
    for i in range(keep_a_ref.shape[0]):
        ref = send_ref if i % 2 else keep_ref
        for d in range(depth):
            ref[i // 2, begun + d] = keep_a_ref[i, d] + got_a_ref[i, d]
            ref[i // 2, depth - begun + d] = keep_b_ref[i, d] + got_b_ref[i, d]


def call(kernel, outs, scratch, specs, out_specs, flops, room=8):
    return pl.pallas_call(
        kernel,
        out_shape=[jax.ShapeDtypeStruct(s, jnp.float32) for s in outs],
        in_specs=specs,
        out_specs=out_specs,
        scratch_shapes=scratch,
        compiler_params=pltpu.CompilerParams(vmem_limit_bytes=room << 20),
        cost_estimate=pl.CostEstimate(flops=flops, bytes_accessed=4 << 20, transcendentals=0),
    )


def in_hbm(array):
    return pltpu.with_memory_space_constraint(array, pltpu.HBM)


def floats(*shapes):
    return [pltpu.VMEM(s, jnp.float32) for s in shapes]


def swaps(tiles, shards, odd_of):
    pairs = []
    for t in range(tiles):
        for s in range(shards):
            other = (t + 1 ^ 1) - 1 if odd_of(s) else t ^ 1
            to = (other, s) if 0 <= other < tiles else (t, spare(s, shards, odd_of))
            pairs.append((t * shards + s, to[0] * shards + to[1]))
    return pairs


def spare(s, shards, odd_of):
    return next((o for o in (s ^ 1, s ^ 2) if o < shards and odd_of(o) == odd_of(s)), s)


def body(
    forward_field,
    adjoint_guess,
    conductivity,
    freq_kappa,
    pair_freq,
    recv_data,
    recv_weights,
    recv_x,
    recv_y,
    recv_z,
):
    pairs, _, layers, size_y, size_z = adjoint_guess.shape
    half = size_y // 2
    count, taps = recv_weights.shape
    tiles = lax.axis_size("tile")
    shards = lax.axis_size("src")
    assert pairs == 1 and layers == SWEEPS and count % UNROLL == 0
    cells = len(HALO_CELLS)
    reach = layers + 2 * (SWEEPS - 1)
    slots = layers + 2 * SWEEPS
    flip = [(i, i ^ 1) for i in range(shards)]

    depth = layers // 2
    piece = (2, depth, half, size_z)
    adj, adj_first, adj_second = call(
        pack_kernel,
        [(2, layers, half, size_z), piece, piece],
        floats((2, layers, size_y, size_z)) + [pltpu.SemaphoreType.DMA((layers,))],
        [HBM],
        [VMEM] * 3,
        1 << 20,
    )(in_hbm(adjoint_guess))
    (cells_out,) = call(
        cells_kernel,
        [(cells, half, size_z)],
        floats((SWEEPS - 1, size_y, size_z)) + [pltpu.SemaphoreType.DMA((1,))],
        [HBM],
        [VMEM],
        1 << 20,
    )(in_hbm(conductivity))
    both = ("tile", "src")
    to_near = swaps(tiles, shards, is_even)
    to_far = swaps(tiles, shards, is_odd)
    far_cells = lax.ppermute(cells_out, both, to_far)
    near_halo = lax.ppermute(adj, both, to_near)
    first_halo = lax.ppermute(adj_first, both, to_far)
    second_halo = lax.ppermute(adj_second, both, to_far)

    source, six_own, cross_own, scale, kappa = call(
        source_kernel,
        [
            (2, 2, reach, half, size_z),
            (2, layers, half, size_z),
            (2, layers, half, size_z),
            (layers, size_y, size_z),
            (8, size_z),
        ],
        [pltpu.SMEM((count,), jnp.int32)] * 3
        + [pltpu.SMEM(freq_kappa.shape, jnp.float32)]
        + floats(
            (taps, count),
            recv_data.shape,
            (layers, size_y, size_z),
            (8 * count, size_z),
            (reach + 8, 2 * size_y, size_z),
        )
        + [pltpu.SemaphoreType.DMA((7,))],
        [HBM] * 4 + [SMEM] + [HBM] * 3,
        [VMEM] * 5,
        1 << 30,
        room=16,
    )(
        in_hbm(recv_x), in_hbm(recv_y), in_hbm(recv_z), in_hbm(freq_kappa), pair_freq,
        in_hbm(recv_weights.T), in_hbm(recv_data), in_hbm(conductivity),
    )

    near_cells = lax.ppermute(far_cells, "src", flip)

    state = (2, 2 * SWEEPS, half + 2 * PAD, size_z)
    weights = (2, slots, half, size_z)
    zero, one, six, cross = call(
        near_kernel, [state, state, weights, weights], [], [VMEM] * 8, [VMEM] * 4, 1 << 26
    )(
        adj, near_halo, far_cells, near_cells, source, six_own, cross_own, kappa
    )

    shard_rows = size_y // shards
    part_shape = (shards // 2, depth, shard_rows, size_z)

    state_zero = (2, depth + SWEEPS - 2, half + 2 * PAD, size_z)
    state_one = (2, depth + SWEEPS, half + 2 * PAD, size_z)

    def far(kernel, *values):
        return call(
            kernel,
            [state_zero, state_one, part_shape, part_shape],
            [],
            [VMEM] * 8,
            [VMEM] * 4,
            1 << 26,
        )(*values, source, six, cross, scale, forward_field)

    zero_a, one_a, send_a, keep_a = far(first_kernel, zero, one, first_halo)
    got_b = lax.ppermute(send_a, "src", flip)
    zero_b, one_b, send_b, keep_b = far(second_kernel, zero_a, one_a, second_halo)
    got_a = lax.ppermute(send_b, "src", flip)

    (field,) = call(
        unpack_kernel,
        [(1, 2, layers, size_y, size_z)],
        floats((2, layers, size_y, size_z)) + [pltpu.SemaphoreType.DMA((layers,))],
        [VMEM] * 5,
        [HBM],
        1 << 20,
    )(zero, zero_a, one_a, zero_b, one_b)

    joined = (shards // 4, layers, shard_rows, size_z)
    send, keep = call(
        join_kernel, [joined, joined], [], [VMEM] * 4, [VMEM] * 2, 1 << 20
    )(keep_a, got_a, keep_b, got_b)
    bit = 2
    while True:
        keep = keep + lax.ppermute(send, "src", [(i, i ^ bit) for i in range(shards)])
        bit *= 2
        if bit == shards:
            break
        send, keep = keep[1::2], keep[0::2]
    return (field, keep[0])


def solution(mesh):
    placed = (
        P(("job", "src"), None, "tile", None, None),
        P(("job", "src"), None, "tile", None, None),
        P(("job", "tile"), None, None),
        P("job"),
        P(("job", "src")),
        P(("job", "src"), None, None),
        P("job", None),
        P("job"),
        P("job"),
        P("job"),
    )
    return jax.shard_map(
        body,
        mesh=mesh,
        in_specs=placed,
        out_specs=(P(("job", "src"), None, "tile", None, None), P(("job", "tile"), "src", None)),
        check_vma=False,
    )
```

```python
import jax
import jax.numpy as jnp
from jax import lax
from jax.experimental import pallas as pl
from jax.experimental.pallas import tpu as pltpu
from jax.sharding import PartitionSpec as P


SWEEPS = 4
COLOURS = tuple(k % 2 for k in range(SWEEPS))
HALO_CELLS = tuple(
    (d, c)
    for d in range(1, SWEEPS)
    for c in (0, 1)
    if any(COLOURS[k] == c and d <= SWEEPS - 1 - k for k in range(SWEEPS))
)
PAD = 8
ROWS = 32
UNROLL = 32
SMEM = pl.BlockSpec(memory_space=pltpu.SMEM)
VMEM = pl.BlockSpec(memory_space=pltpu.VMEM)
HBM = pl.BlockSpec(memory_space=pltpu.HBM)


def odd_lanes(shift, rows, cols):
    return ((lax.broadcasted_iota(jnp.int32, (rows, cols), 1) + shift) & 1) == 1


def of_colour(colour, odd, even_rows, odd_rows):
    if colour == 0:
        return jnp.where(odd, odd_rows, even_rows)
    return jnp.where(odd, even_rows, odd_rows)


def coefficients(kappa, conductivity):
    coupling = kappa * conductivity
    inverse = 1.0 / (36.0 + coupling * coupling)
    return 6.0 * inverse, coupling * inverse


def is_odd(shard):
    return shard % 2 == 1


def is_even(shard):
    return shard % 2 == 0


def near_on_right():
    return (lax.axis_index("tile") % 2 == 0) == is_odd(lax.axis_index("src"))


def layer_of(slot, layers):
    ahead = slot - SWEEPS
    return jnp.where(near_on_right(), layers - 1 - ahead, ahead)


def start_all(copies):
    for copy in copies:
        copy.start()
    return copies


def pack_kernel(guess_hbm, adj_ref, first_ref, second_ref, guess_ref, sems):
    _, layers, half, size_z = adj_ref.shape
    rows = min(ROWS, half)
    first = lax.axis_index("tile") * layers
    depth = first_ref.shape[1]
    copies = start_all(
        [
            pltpu.make_async_copy(guess_hbm.at[0, :, i], guess_ref.at[:, i], sems.at[i])
            for i in range(layers)
        ]
    )
    for layer in range(layers):
        odd = odd_lanes(first + layer, rows, size_z)
        copies[layer].wait()
        for part in range(2):
            for r in range(0, half, rows):
                a = guess_ref[part, layer, pl.ds(2 * r, rows, stride=2), :]
                b = guess_ref[part, layer, pl.ds(2 * r + 1, rows, stride=2), :]
                adj_ref[part, layer, pl.ds(r, rows), :] = of_colour(1, odd, a, b)
    for d in range(SWEEPS):
        layer = layer_of(SWEEPS + layers - 1 - d, layers)
        ref = (first_ref, second_ref)[d // depth]
        for part in range(2):
            ref[part, d % depth] = adj_ref[part, layer]


def cells_kernel(cond_hbm, cells_ref, cond_ref, sems):
    layers = cond_hbm.shape[0]
    deep, size_y, size_z = cond_ref.shape
    half = size_y // 2
    rows = min(ROWS, half)
    to_right = jnp.logical_not(near_on_right())
    base = jnp.where(to_right, layers - deep, 0)
    copy = pltpu.make_async_copy(cond_hbm.at[pl.ds(base, deep)], cond_ref, sems.at[0])
    copy.start()
    copy.wait()
    first = lax.axis_index("tile") * layers + base
    for i, (d, c) in enumerate(HALO_CELLS):
        layer = jnp.where(to_right, deep - d, d - 1)
        odd = odd_lanes(first + layer, rows, size_z)
        for r in range(0, half, rows):
            a = cond_ref[layer, pl.ds(2 * r, rows, stride=2), :]
            b = cond_ref[layer, pl.ds(2 * r + 1, rows, stride=2), :]
            cells_ref[i, pl.ds(r, rows), :] = of_colour(c, odd, a, b)


def source_kernel(
    x_hbm, y_hbm, z_hbm, kappas_hbm, freq_ref, weight_hbm, data_hbm, cond_hbm,
    source_ref, six_ref, cross_ref, scale_ref, kappa_ref,
    x_ref, y_ref, z_ref, kappas_ref, weight_ref, data_ref, cond_ref,
    terms_ref, total_ref, sems,
):
    layers, size_y, size_z = cond_ref.shape
    half = size_y // 2
    rows = min(ROWS, half)
    taps, count = weight_ref.shape
    reach = source_ref.shape[2]
    halo = SWEEPS - 1
    first = lax.axis_index("tile") * layers
    copies = start_all(
        [
            pltpu.make_async_copy(a, b, sems.at[i])
            for i, (a, b) in enumerate(
                (
                    (x_hbm, x_ref), (y_hbm, y_ref), (z_hbm, z_ref), (kappas_hbm, kappas_ref),
                    (weight_hbm, weight_ref), (data_hbm, data_ref),
                    (cond_hbm, cond_ref),
                )
            )
        ]
    )
    for layer in range(reach):
        total_ref[4 + layer] = jnp.zeros(total_ref.shape[1:], jnp.float32)
    for copy in copies:
        copy.wait()
    kappa = kappas_ref[freq_ref[0]]
    kappa_ref[...] = jnp.full(kappa_ref.shape, kappa, jnp.float32)

    blank = jnp.zeros((size_z - taps, count), jnp.float32)
    weights = weight_ref[...]
    for c in range(2):
        terms = jnp.concatenate([weights * data_ref[0, c : c + 1, :], blank], axis=0).T
        for b in range(4):
            moved = pltpu.roll(terms, size_z - 4 * b, 1) if b else terms
            terms_ref[pl.ds(2 * b + c, count, stride=8), :] = moved

    lane = lax.broadcasted_iota(jnp.int32, (8, size_z), 1)

    def add_block(r):
        z = z_ref[r]
        base = jnp.clip(x_ref[r] - first + halo, -4, reach) + 4
        row = 2 * y_ref[r]
        inside = (lane - z).astype(jnp.uint32) < 4
        first_tap = pltpu.roll(terms_ref[pl.ds(pl.multiple_of(8 * r, 8), 8), :], z, 1)
        terms = []
        for a in range(4):
            moved = pltpu.roll(first_tap, size_z - 16 * a, 1) if a else first_tap
            terms.append(jnp.where(inside, moved, 0.0))
        old = [total_ref[base + a, pl.ds(row, 8), :] for a in range(4)]
        for a in range(4):
            total_ref[base + a, pl.ds(row, 8), :] = old[a] + terms[a]

    def some_blocks(step, carry):
        for u in range(UNROLL):
            add_block(step * UNROLL + u)
        return carry

    lax.fori_loop(0, count // UNROLL, some_blocks, 0)

    for ahead in range(layers):
        layer = layer_of(SWEEPS + ahead, layers)
        odd = odd_lanes(first + layer, rows, size_z)
        for r in range(0, half, rows):
            a = cond_ref[layer, pl.ds(2 * r, rows, stride=2), :]
            b = cond_ref[layer, pl.ds(2 * r + 1, rows, stride=2), :]
            for c in (0, 1):
                six, cross = coefficients(kappa, of_colour(c, odd, a, b))
                six_ref[c, ahead, pl.ds(r, rows), :] = six
                cross_ref[c, ahead, pl.ds(r, rows), :] = cross
        scale_ref[ahead] = -(kappa * cond_ref[layer])

    def pack_layer(i, carry):
        layer = layer_of(i + 1, layers)
        odd = odd_lanes(first + layer, rows, size_z)
        for part in range(2):
            for r in range(0, half, rows):
                a = total_ref[4 + halo + layer, pl.ds(4 * r + part, rows, stride=4), :]
                b = total_ref[4 + halo + layer, pl.ds(4 * r + 2 + part, rows, stride=4), :]
                for c in (0, 1):
                    source_ref[c, part, i, pl.ds(r, rows), :] = of_colour(c, odd, a, b)
        return carry

    lax.fori_loop(0, reach, pack_layer, 0)


class Sweeper:
    def __init__(self, half, size_z, layers, source, six, cross):
        self.half, self.size_z = half, size_z
        self.source, self.six, self.cross = source, six, cross
        self.where = ({}, {})
        first = lax.axis_index("tile") * layers
        self.rows = min(ROWS, half)
        base = first + jnp.where(near_on_right(), layers - 1, 0)
        self.odd = odd_lanes(base, self.rows, size_z)
        lane = lax.broadcasted_iota(jnp.int32, (self.rows, size_z), 1)
        self.after, self.before = lane > 0, lane < size_z - 1
        near = lax.broadcasted_iota(jnp.int32, (size_z, size_z), 0)
        near = jnp.abs(near - lax.broadcasted_iota(jnp.int32, (size_z, size_z), 1)) <= 1
        near = jnp.where(near, 1.0, 0.0).astype(jnp.bfloat16)
        self.near = jnp.concatenate([near] * 3, axis=0)

    def along_z(self, values):
        high = values.astype(jnp.bfloat16)
        rest = values - high.astype(jnp.float32)
        middle = rest.astype(jnp.bfloat16)
        low = (rest - middle.astype(jnp.float32)).astype(jnp.bfloat16)
        pieces = jnp.concatenate([high, middle, low], axis=1)
        return jnp.dot(pieces, self.near, preferred_element_type=jnp.float32)

    def sums(self, c, part, slot):
        old = self.where[1 - c]
        (here, at_here), (left, at_left), (right, at_right) = old[slot], old[slot - 1], old[slot + 1]
        rows = self.rows
        by_matrix = part == 1
        if by_matrix:
            beside = self.along_z(here[part, at_here, pl.ds(PAD, self.half), :])
        out = []
        for r in range(0, self.half, rows):
            above = here[part, at_here, pl.ds(PAD + r + 1, rows), :]
            below = here[part, at_here, pl.ds(PAD + r - 1, rows), :]
            if (slot + c) % 2:
                above, below = below, above
            total = left[part, at_left, pl.ds(PAD + r, rows), :]
            total += right[part, at_right, pl.ds(PAD + r, rows), :]
            total += jnp.where(self.odd, above, below)
            if by_matrix:
                total += beside[r : r + rows]
            else:
                centre = here[part, at_here, pl.ds(PAD + r, rows), :]
                total += centre
                total += jnp.where(self.after, pltpu.roll(centre, 1, 1), 0.0)
                total += jnp.where(self.before, pltpu.roll(centre, self.size_z - 1, 1), 0.0)
            out.append(total + self.source[c, part, slot - 1, pl.ds(r, rows), :])
        return out

    def update(self, c, slot, new, index):
        sums = [self.sums(c, part, slot) for part in range(2)]
        for i, r in enumerate(range(0, self.half, self.rows)):
            six = self.six[c, slot, pl.ds(r, self.rows), :]
            cross = self.cross[c, slot, pl.ds(r, self.rows), :]
            at = pl.ds(PAD + r, self.rows)
            new[0, index, at, :] = six * sums[0][i] + cross * sums[1][i]
            new[1, index, at, :] = six * sums[1][i] - cross * sums[0][i]
        self.where[c][slot] = (new, index)


def clear_edges(ref, slots, half):
    edge = jnp.zeros((PAD, ref.shape[-1]), jnp.float32)
    for part in range(2):
        for slot in slots:
            ref[part, slot, pl.ds(0, PAD), :] = edge
            ref[part, slot, pl.ds(PAD + half, PAD), :] = edge


def near_kernel(
    adj_ref, halo_ref, far_cells_ref, near_cells_ref,
    source_ref, six_own_ref, cross_own_ref, kappa_ref,
    zero_ref, one_ref, six_ref, cross_ref,
):
    _, layers, half, size_z = adj_ref.shape
    tile, tiles = lax.axis_index("tile"), lax.axis_size("tile")
    on_right = near_on_right()
    rows = min(ROWS, half)
    reached = layers + SWEEPS
    is_last, is_first = tile == tiles - 1, tile == 0
    clear_edges(zero_ref, range(1, reached - 1), half)
    clear_edges(one_ref, range(reached), half)
    for part in range(2):
        for slot in range(reached):
            layer = layer_of(slot, layers)
            if slot < SWEEPS:
                values = halo_ref[part, jnp.where(on_right, layer - layers, layer + SWEEPS)]
                values = jnp.where(jnp.where(on_right, is_last, is_first), 0.0, values)
            else:
                values = adj_ref[part, layer]
            one_ref[part, slot, pl.ds(PAD, half), :] = values
    for c in (0, 1):
        for layer in range(layers):
            six_ref[c, SWEEPS + layer] = six_own_ref[c, layer]
            cross_ref[c, SWEEPS + layer] = cross_own_ref[c, layer]
    kappa = jnp.broadcast_to(kappa_ref[0:1, :], (rows, size_z))
    for ref, is_near in ((near_cells_ref, True), (far_cells_ref, False)):
        missing = jnp.where(on_right, is_last, is_first)
        if not is_near:
            missing = jnp.where(on_right, is_first, is_last)
        there = jnp.where(missing, 0.0, 1.0)
        for i, (d, c) in enumerate(HALO_CELLS):
            slot = SWEEPS - d if is_near else SWEEPS + layers - 1 + d
            for r in range(0, half, rows):
                six, cross = coefficients(kappa, ref[i, pl.ds(r, rows), :])
                six_ref[c, slot, pl.ds(r, rows), :] = six * there
                cross_ref[c, slot, pl.ds(r, rows), :] = cross * there
    sweeper = Sweeper(half, size_z, layers, source_ref, six_ref, cross_ref)
    sweeper.where[1].update({slot: (one_ref, slot) for slot in range(reached)})
    for k, c in enumerate(COLOURS):
        for slot in range(1 + k, reached - 1 - k):
            sweeper.update(c, slot, (zero_ref, one_ref)[c], slot)


def gradient_terms(slots, zeros, ones, scale_ref, forward_ref, send_ref, keep_ref):
    layers, size_y, size_z = scale_ref.shape
    shards = 2 * send_ref.shape[0]
    shard = lax.axis_index("src")
    shard_rows = size_y // shards
    rows = min(ROWS, shard_rows // 2)
    for slot in slots:
        layer = layer_of(slot, layers)
        swap = odd_lanes(lax.axis_index("tile") * layers + layer, rows, size_z)
        for m in range(shards):
            ref = send_ref if m % 2 else keep_ref
            start = (shard ^ m) * shard_rows
            for r in range(0, shard_rows // 2, rows):
                at = pl.ds(pl.multiple_of(PAD + start // 2 + r, PAD), rows)
                a, b = (
                    [ref[part, i, at, :] for part in range(2)]
                    for ref, i in (zeros[slot], ones[slot])
                )
                for second in range(2):
                    if second:
                        a, b = b, a
                    field = [jnp.where(swap, b[part], a[part]) for part in range(2)]
                    cells = pl.ds(pl.multiple_of(start + 2 * r, 2 * rows) + second, rows, stride=2)
                    products = forward_ref[0, 0, layer, cells, :] * field[1]
                    products += forward_ref[0, 1, layer, cells, :] * field[0]
                    into = pl.ds(2 * r + second, rows, stride=2)
                    ref[m // 2, layer % len(slots), into, :] = (
                        scale_ref[slot - SWEEPS, cells, :] * products
                    )


def far_sweeps(begin, depth, halo_ref, source_ref, six_ref, cross_ref, scale_ref, older, zero_ref, one_ref):
    layers, size_y, size_z = scale_ref.shape
    half = size_y // 2
    tile, tiles = lax.axis_index("tile"), lax.axis_size("tile")
    missing = jnp.where(near_on_right(), tile == 0, tile == tiles - 1)
    bases = (begin - SWEEPS + 1, begin - SWEEPS)
    clear_edges(zero_ref, range(zero_ref.shape[1]), half)
    clear_edges(one_ref, range(one_ref.shape[1]), half)
    for part in range(2):
        for d in range(depth):
            values = jnp.where(missing, 0.0, halo_ref[part, d])
            one_ref[part, begin + d - bases[1], pl.ds(PAD, half), :] = values
    sweeper = Sweeper(half, size_z, layers, source_ref, six_ref, cross_ref)
    for c in (0, 1):
        sweeper.where[c].update(older[c])
    sweeper.where[1].update({begin + d: (one_ref, begin + d - bases[1]) for d in range(depth)})
    for k, c in enumerate(COLOURS):
        for slot in range(begin - 1 - k, begin + depth - 1 - k):
            sweeper.update(c, slot, (zero_ref, one_ref)[c], slot - bases[c])
    return sweeper.where


def near_values(zero_ref, one_ref):
    reached = 2 * SWEEPS
    return (
        {slot: (zero_ref, slot) for slot in range(1, reached - 1)},
        {slot: (one_ref, slot) for slot in range(reached)},
    )


def first_kernel(
    zero_in_ref, one_in_ref, halo_ref, source_ref, six_ref, cross_ref, scale_ref, forward_ref,
    zero_ref, one_ref, send_ref, keep_ref,
):
    depth = halo_ref.shape[1]
    zeros, ones = far_sweeps(
        2 * SWEEPS, depth, halo_ref, source_ref, six_ref, cross_ref, scale_ref,
        near_values(zero_in_ref, one_in_ref), zero_ref, one_ref,
    )
    done = range(SWEEPS, SWEEPS + depth)
    gradient_terms(done, zeros, ones, scale_ref, forward_ref, send_ref, keep_ref)


def second_kernel(
    zero_in_ref, one_in_ref, halo_ref, source_ref, six_ref, cross_ref, scale_ref, forward_ref,
    zero_ref, one_ref, send_ref, keep_ref,
):
    depth = halo_ref.shape[1]
    begin = 2 * SWEEPS + depth
    older = (
        {SWEEPS + 1 + i: (zero_in_ref, i) for i in range(zero_in_ref.shape[1])},
        {SWEEPS + i: (one_in_ref, i) for i in range(one_in_ref.shape[1])},
    )
    zeros, ones = far_sweeps(
        begin, depth, halo_ref, source_ref, six_ref, cross_ref, scale_ref, older, zero_ref, one_ref
    )
    done = range(SWEEPS + depth, SWEEPS + 2 * depth)
    gradient_terms(done, zeros, ones, scale_ref, forward_ref, send_ref, keep_ref)


def unpack_kernel(near_ref, zero_a_ref, one_a_ref, zero_b_ref, one_b_ref, out_hbm, out_ref, sems):
    _, layers, size_y, size_z = out_ref.shape
    depth = layers // 2
    zeros = [(near_ref, SWEEPS)] + [(zero_a_ref, i) for i in range(depth)]
    zeros += [(zero_b_ref, i) for i in range(depth - 1)]
    ones = [(ref, i) for ref in (one_a_ref, one_b_ref) for i in range(depth)]
    half = size_y // 2
    rows = min(ROWS, half)
    first = lax.axis_index("tile") * layers
    copies = []
    for slot in range(SWEEPS, SWEEPS + layers):
        layer = layer_of(slot, layers)
        odd = odd_lanes(first + layer, rows, size_z)
        for part in range(2):
            for r in range(0, half, rows):
                a = zeros[slot - SWEEPS][0][part, zeros[slot - SWEEPS][1], pl.ds(PAD + r, rows), :]
                b = ones[slot - SWEEPS][0][part, ones[slot - SWEEPS][1], pl.ds(PAD + r, rows), :]
                out_ref[part, slot - SWEEPS, pl.ds(2 * r, rows, stride=2), :] = jnp.where(odd, b, a)
                out_ref[part, slot - SWEEPS, pl.ds(2 * r + 1, rows, stride=2), :] = jnp.where(odd, a, b)
        i = slot - SWEEPS
        copies.append(
            pltpu.make_async_copy(out_ref.at[:, i], out_hbm.at[0, :, layer], sems.at[i])
        )
        copies[-1].start()
    for copy in copies:
        copy.wait()


def join_kernel(keep_in_ref, got_ref, send_ref, keep_ref):
    for i in range(keep_in_ref.shape[0]):
        ref = send_ref if i % 2 else keep_ref
        ref[i // 2] = keep_in_ref[i] + got_ref[i]


def finish_kernel(begun_ref, begun_got_ref, ended_ref, ended_got_ref, out_ref):
    depth = begun_ref.shape[1]
    base = jnp.where(near_on_right(), depth, 0)
    for d in range(depth):
        out_ref[base + d] = begun_ref[0, d] + begun_got_ref[0, d]
        out_ref[depth - base + d] = ended_ref[0, d] + ended_got_ref[0, d]


def call(kernel, outs, scratch, specs, out_specs, flops, room=8):
    return pl.pallas_call(
        kernel,
        out_shape=[jax.ShapeDtypeStruct(s, jnp.float32) for s in outs],
        in_specs=specs,
        out_specs=out_specs,
        scratch_shapes=scratch,
        compiler_params=pltpu.CompilerParams(vmem_limit_bytes=room << 20),
        cost_estimate=pl.CostEstimate(flops=flops, bytes_accessed=4 << 20, transcendentals=0),
    )


def in_hbm(array):
    return pltpu.with_memory_space_constraint(array, pltpu.HBM)


def floats(*shapes):
    return [pltpu.VMEM(s, jnp.float32) for s in shapes]


def swaps(tiles, shards, odd_of):
    pairs = []
    for t in range(tiles):
        for s in range(shards):
            other = (t + 1 ^ 1) - 1 if odd_of(s) else t ^ 1
            to = (other, s) if 0 <= other < tiles else (t, spare(s, shards, odd_of))
            pairs.append((t * shards + s, to[0] * shards + to[1]))
    return pairs


def spare(s, shards, odd_of):
    return next((o for o in (s ^ 1, s ^ 2) if o < shards and odd_of(o) == odd_of(s)), s)


def body(
    forward_field,
    adjoint_guess,
    conductivity,
    freq_kappa,
    pair_freq,
    recv_data,
    recv_weights,
    recv_x,
    recv_y,
    recv_z,
):
    pairs, _, layers, size_y, size_z = adjoint_guess.shape
    half = size_y // 2
    count, taps = recv_weights.shape
    tiles = lax.axis_size("tile")
    shards = lax.axis_size("src")
    assert pairs == 1 and layers == SWEEPS and count % UNROLL == 0
    cells = len(HALO_CELLS)
    reach = layers + 2 * (SWEEPS - 1)
    slots = layers + 2 * SWEEPS
    flip = [(i, i ^ 1) for i in range(shards)]

    depth = layers // 2
    piece = (2, depth, half, size_z)
    adj, adj_first, adj_second = call(
        pack_kernel,
        [(2, layers, half, size_z), piece, piece],
        floats((2, layers, size_y, size_z)) + [pltpu.SemaphoreType.DMA((layers,))],
        [HBM],
        [VMEM] * 3,
        1 << 20,
    )(in_hbm(adjoint_guess))
    (cells_out,) = call(
        cells_kernel,
        [(cells, half, size_z)],
        floats((SWEEPS - 1, size_y, size_z)) + [pltpu.SemaphoreType.DMA((1,))],
        [HBM],
        [VMEM],
        1 << 20,
    )(in_hbm(conductivity))
    both = ("tile", "src")
    to_near = swaps(tiles, shards, is_even)
    to_far = swaps(tiles, shards, is_odd)
    far_cells = lax.ppermute(cells_out, both, to_far)
    near_halo = lax.ppermute(adj, both, to_near)
    first_halo = lax.ppermute(adj_first, both, to_far)
    second_halo = lax.ppermute(adj_second, both, to_far)

    source, six_own, cross_own, scale, kappa = call(
        source_kernel,
        [
            (2, 2, reach, half, size_z),
            (2, layers, half, size_z),
            (2, layers, half, size_z),
            (layers, size_y, size_z),
            (8, size_z),
        ],
        [pltpu.SMEM((count,), jnp.int32)] * 3
        + [pltpu.SMEM(freq_kappa.shape, jnp.float32)]
        + floats(
            (taps, count),
            recv_data.shape,
            (layers, size_y, size_z),
            (8 * count, size_z),
            (reach + 8, 2 * size_y, size_z),
        )
        + [pltpu.SemaphoreType.DMA((7,))],
        [HBM] * 4 + [SMEM] + [HBM] * 3,
        [VMEM] * 5,
        1 << 30,
        room=16,
    )(
        in_hbm(recv_x), in_hbm(recv_y), in_hbm(recv_z), in_hbm(freq_kappa), pair_freq,
        in_hbm(recv_weights.T), in_hbm(recv_data), in_hbm(conductivity),
    )

    near_cells = lax.ppermute(far_cells, "src", flip)

    state = (2, 2 * SWEEPS, half + 2 * PAD, size_z)
    weights = (2, slots, half, size_z)
    zero, one, six, cross = call(
        near_kernel, [state, state, weights, weights], [], [VMEM] * 8, [VMEM] * 4, 1 << 26
    )(
        adj, near_halo, far_cells, near_cells, source, six_own, cross_own, kappa
    )

    shard_rows = size_y // shards
    part_shape = (shards // 2, depth, shard_rows, size_z)

    state_zero = (2, depth + SWEEPS - 2, half + 2 * PAD, size_z)
    state_one = (2, depth + SWEEPS, half + 2 * PAD, size_z)

    def far(kernel, *values):
        return call(
            kernel,
            [state_zero, state_one, part_shape, part_shape],
            [],
            [VMEM] * 8,
            [VMEM] * 4,
            1 << 26,
        )(*values, source, six, cross, scale, forward_field)

    zero_a, one_a, send_a, keep_a = far(first_kernel, zero, one, first_halo)
    got_b = lax.ppermute(send_a, "src", flip)
    zero_b, one_b, send_b, keep_b = far(second_kernel, zero_a, one_a, second_halo)
    got_a = lax.ppermute(send_b, "src", flip)

    (field,) = call(
        unpack_kernel,
        [(1, 2, layers, size_y, size_z)],
        floats((2, layers, size_y, size_z)) + [pltpu.SemaphoreType.DMA((layers,))],
        [VMEM] * 5,
        [HBM],
        1 << 20,
    )(zero, zero_a, one_a, zero_b, one_b)

    def join(keep, got):
        joined = (shards // 4, depth, shard_rows, size_z)
        return call(join_kernel, [joined, joined], [], [VMEM] * 2, [VMEM] * 2, 1 << 20)(keep, got)

    def add_up(send, keep):
        bit = 2
        while True:
            got = lax.ppermute(send, "src", [(i, i ^ bit) for i in range(shards)])
            bit *= 2
            if bit == shards:
                return keep, got
            keep = keep + got
            send, keep = keep[1::2], keep[0::2]

    ended = add_up(*join(keep_b, got_b))
    begun = add_up(*join(keep_a, got_a))
    (gradient,) = call(
        finish_kernel, [(layers, shard_rows, size_z)], [], [VMEM] * 4, [VMEM], 1 << 20
    )(*begun, *ended)
    return (field, gradient)


def solution(mesh):
    placed = (
        P(("job", "src"), None, "tile", None, None),
        P(("job", "src"), None, "tile", None, None),
        P(("job", "tile"), None, None),
        P("job"),
        P(("job", "src")),
        P(("job", "src"), None, None),
        P("job", None),
        P("job"),
        P("job"),
        P("job"),
    )
    return jax.shard_map(
        body,
        mesh=mesh,
        in_specs=placed,
        out_specs=(P(("job", "src"), None, "tile", None, None), P(("job", "tile"), "src", None)),
        check_vma=False,
    )
```

```python
import jax
import jax.numpy as jnp
from jax import lax
from jax.experimental import pallas as pl
from jax.experimental.pallas import tpu as pltpu
from jax.sharding import PartitionSpec as P


SWEEPS = 4
COLOURS = tuple(k % 2 for k in range(SWEEPS))
HALO_CELLS = tuple(
    (d, c)
    for d in range(1, SWEEPS)
    for c in (0, 1)
    if any(COLOURS[k] == c and d <= SWEEPS - 1 - k for k in range(SWEEPS))
)
PAD = 8
ROWS = 32
UNROLL = 32
SMEM = pl.BlockSpec(memory_space=pltpu.SMEM)
VMEM = pl.BlockSpec(memory_space=pltpu.VMEM)
HBM = pl.BlockSpec(memory_space=pltpu.HBM)


def odd_lanes(shift, rows, cols):
    return ((lax.broadcasted_iota(jnp.int32, (rows, cols), 1) + shift) & 1) == 1


def of_colour(colour, odd, even_rows, odd_rows):
    if colour == 0:
        return jnp.where(odd, odd_rows, even_rows)
    return jnp.where(odd, even_rows, odd_rows)


def coefficients(kappa, conductivity):
    coupling = kappa * conductivity
    inverse = 1.0 / (36.0 + coupling * coupling)
    return 6.0 * inverse, coupling * inverse


def is_odd(shard):
    return shard % 2 == 1


def is_even(shard):
    return shard % 2 == 0


def near_on_right():
    return (lax.axis_index("tile") % 2 == 0) == is_odd(lax.axis_index("src"))


def layer_of(slot, layers):
    ahead = slot - SWEEPS
    return jnp.where(near_on_right(), layers - 1 - ahead, ahead)


def start_all(copies):
    for copy in copies:
        copy.start()
    return copies


def pack_kernel(guess_hbm, adj_ref, first_ref, second_ref, guess_ref, sems):
    _, layers, half, size_z = adj_ref.shape
    rows = min(ROWS, half)
    first = lax.axis_index("tile") * layers
    depth = first_ref.shape[1]
    copies = start_all(
        [
            pltpu.make_async_copy(guess_hbm.at[0, :, i], guess_ref.at[:, i], sems.at[i])
            for i in range(layers)
        ]
    )
    for layer in range(layers):
        odd = odd_lanes(first + layer, rows, size_z)
        copies[layer].wait()
        for part in range(2):
            for r in range(0, half, rows):
                a = guess_ref[part, layer, pl.ds(2 * r, rows, stride=2), :]
                b = guess_ref[part, layer, pl.ds(2 * r + 1, rows, stride=2), :]
                adj_ref[part, layer, pl.ds(r, rows), :] = of_colour(1, odd, a, b)
    for d in range(SWEEPS):
        layer = layer_of(SWEEPS + layers - 1 - d, layers)
        ref = (first_ref, second_ref)[d // depth]
        for part in range(2):
            ref[part, d % depth] = adj_ref[part, layer]


def cells_kernel(cond_hbm, cells_ref, cond_ref, sems):
    layers = cond_hbm.shape[0]
    deep, size_y, size_z = cond_ref.shape
    half = size_y // 2
    rows = min(ROWS, half)
    to_right = jnp.logical_not(near_on_right())
    base = jnp.where(to_right, layers - deep, 0)
    copy = pltpu.make_async_copy(cond_hbm.at[pl.ds(base, deep)], cond_ref, sems.at[0])
    copy.start()
    copy.wait()
    first = lax.axis_index("tile") * layers + base
    for i, (d, c) in enumerate(HALO_CELLS):
        layer = jnp.where(to_right, deep - d, d - 1)
        odd = odd_lanes(first + layer, rows, size_z)
        for r in range(0, half, rows):
            a = cond_ref[layer, pl.ds(2 * r, rows, stride=2), :]
            b = cond_ref[layer, pl.ds(2 * r + 1, rows, stride=2), :]
            cells_ref[i, pl.ds(r, rows), :] = of_colour(c, odd, a, b)


def source_kernel(
    x_hbm, y_hbm, z_hbm, kappas_hbm, freq_ref, weight_hbm, data_hbm, cond_hbm,
    source_ref, six_ref, cross_ref, scale_ref, kappa_ref,
    x_ref, y_ref, z_ref, kappas_ref, weight_ref, data_ref, cond_ref,
    terms_ref, total_ref, sems,
):
    layers, size_y, size_z = cond_ref.shape
    half = size_y // 2
    rows = min(ROWS, half)
    taps, count = weight_ref.shape
    reach = source_ref.shape[2]
    halo = SWEEPS - 1
    first = lax.axis_index("tile") * layers
    copies = start_all(
        [
            pltpu.make_async_copy(a, b, sems.at[i])
            for i, (a, b) in enumerate(
                (
                    (x_hbm, x_ref), (y_hbm, y_ref), (z_hbm, z_ref), (kappas_hbm, kappas_ref),
                    (weight_hbm, weight_ref), (data_hbm, data_ref),
                    (cond_hbm, cond_ref),
                )
            )
        ]
    )
    for layer in range(reach):
        total_ref[4 + layer] = jnp.zeros(total_ref.shape[1:], jnp.float32)
    for copy in copies:
        copy.wait()
    kappa = kappas_ref[freq_ref[0]]
    kappa_ref[...] = jnp.full(kappa_ref.shape, kappa, jnp.float32)

    blank = jnp.zeros((size_z - taps, count), jnp.float32)
    weights = weight_ref[...]
    for c in range(2):
        terms = jnp.concatenate([weights * data_ref[0, c : c + 1, :], blank], axis=0).T
        for b in range(4):
            moved = pltpu.roll(terms, size_z - 4 * b, 1) if b else terms
            terms_ref[pl.ds(2 * b + c, count, stride=8), :] = moved

    lane = lax.broadcasted_iota(jnp.int32, (8, size_z), 1)

    def add_block(r):
        z = z_ref[r]
        base = jnp.clip(x_ref[r] - first + halo, -4, reach) + 4
        row = 2 * y_ref[r]
        inside = (lane - z).astype(jnp.uint32) < 4
        first_tap = pltpu.roll(terms_ref[pl.ds(pl.multiple_of(8 * r, 8), 8), :], z, 1)
        terms = []
        for a in range(4):
            moved = pltpu.roll(first_tap, size_z - 16 * a, 1) if a else first_tap
            terms.append(jnp.where(inside, moved, 0.0))
        old = [total_ref[base + a, pl.ds(row, 8), :] for a in range(4)]
        for a in range(4):
            total_ref[base + a, pl.ds(row, 8), :] = old[a] + terms[a]

    def some_blocks(step, carry):
        for u in range(UNROLL):
            add_block(step * UNROLL + u)
        return carry

    lax.fori_loop(0, count // UNROLL, some_blocks, 0)

    for ahead in range(layers):
        layer = layer_of(SWEEPS + ahead, layers)
        odd = odd_lanes(first + layer, rows, size_z)
        for r in range(0, half, rows):
            a = cond_ref[layer, pl.ds(2 * r, rows, stride=2), :]
            b = cond_ref[layer, pl.ds(2 * r + 1, rows, stride=2), :]
            for c in (0, 1):
                six, cross = coefficients(kappa, of_colour(c, odd, a, b))
                six_ref[c, ahead, pl.ds(r, rows), :] = six
                cross_ref[c, ahead, pl.ds(r, rows), :] = cross
        scale_ref[ahead] = -(kappa * cond_ref[layer])

    def pack_layer(i, carry):
        layer = layer_of(i + 1, layers)
        odd = odd_lanes(first + layer, rows, size_z)
        for part in range(2):
            for r in range(0, half, rows):
                a = total_ref[4 + halo + layer, pl.ds(4 * r + part, rows, stride=4), :]
                b = total_ref[4 + halo + layer, pl.ds(4 * r + 2 + part, rows, stride=4), :]
                for c in (0, 1):
                    source_ref[c, part, i, pl.ds(r, rows), :] = of_colour(c, odd, a, b)
        return carry

    lax.fori_loop(0, reach, pack_layer, 0)


class Sweeper:
    def __init__(self, half, size_z, layers, source, six, cross):
        self.half, self.size_z = half, size_z
        self.source, self.six, self.cross = source, six, cross
        self.where = ({}, {})
        first = lax.axis_index("tile") * layers
        self.rows = min(ROWS, half)
        base = first + jnp.where(near_on_right(), layers - 1, 0)
        self.odd = odd_lanes(base, self.rows, size_z)
        lane = lax.broadcasted_iota(jnp.int32, (self.rows, size_z), 1)
        self.after, self.before = lane > 0, lane < size_z - 1
        near = lax.broadcasted_iota(jnp.int32, (size_z, size_z), 0)
        near = jnp.abs(near - lax.broadcasted_iota(jnp.int32, (size_z, size_z), 1)) <= 1
        near = jnp.where(near, 1.0, 0.0).astype(jnp.bfloat16)
        self.near = jnp.concatenate([near] * 3, axis=0)

    def along_z(self, values):
        high = values.astype(jnp.bfloat16)
        rest = values - high.astype(jnp.float32)
        middle = rest.astype(jnp.bfloat16)
        low = (rest - middle.astype(jnp.float32)).astype(jnp.bfloat16)
        pieces = jnp.concatenate([high, middle, low], axis=1)
        return jnp.dot(pieces, self.near, preferred_element_type=jnp.float32)

    def sums(self, c, part, slot):
        old = self.where[1 - c]
        (here, at_here), (left, at_left), (right, at_right) = old[slot], old[slot - 1], old[slot + 1]
        rows = self.rows
        by_matrix = part == 1
        if by_matrix:
            beside = self.along_z(here[part, at_here, pl.ds(PAD, self.half), :])
        out = []
        for r in range(0, self.half, rows):
            above = here[part, at_here, pl.ds(PAD + r + 1, rows), :]
            below = here[part, at_here, pl.ds(PAD + r - 1, rows), :]
            if (slot + c) % 2:
                above, below = below, above
            total = left[part, at_left, pl.ds(PAD + r, rows), :]
            total += right[part, at_right, pl.ds(PAD + r, rows), :]
            total += jnp.where(self.odd, above, below)
            if by_matrix:
                total += beside[r : r + rows]
            else:
                centre = here[part, at_here, pl.ds(PAD + r, rows), :]
                total += centre
                total += jnp.where(self.after, pltpu.roll(centre, 1, 1), 0.0)
                total += jnp.where(self.before, pltpu.roll(centre, self.size_z - 1, 1), 0.0)
            out.append(total + self.source[c, part, slot - 1, pl.ds(r, rows), :])
        return out

    def update(self, c, slot, new, index):
        sums = [self.sums(c, part, slot) for part in range(2)]
        for i, r in enumerate(range(0, self.half, self.rows)):
            six = self.six[c, slot, pl.ds(r, self.rows), :]
            cross = self.cross[c, slot, pl.ds(r, self.rows), :]
            at = pl.ds(PAD + r, self.rows)
            new[0, index, at, :] = six * sums[0][i] + cross * sums[1][i]
            new[1, index, at, :] = six * sums[1][i] - cross * sums[0][i]
        self.where[c][slot] = (new, index)


def clear_edges(ref, slots, half):
    edge = jnp.zeros((PAD, ref.shape[-1]), jnp.float32)
    for part in range(2):
        for slot in slots:
            ref[part, slot, pl.ds(0, PAD), :] = edge
            ref[part, slot, pl.ds(PAD + half, PAD), :] = edge


def near_kernel(
    adj_ref, halo_ref, far_cells_ref, near_cells_ref,
    source_ref, six_own_ref, cross_own_ref, kappa_ref,
    zero_ref, one_ref, six_ref, cross_ref,
):
    _, layers, half, size_z = adj_ref.shape
    tile, tiles = lax.axis_index("tile"), lax.axis_size("tile")
    on_right = near_on_right()
    rows = min(ROWS, half)
    reached = layers + SWEEPS
    is_last, is_first = tile == tiles - 1, tile == 0
    clear_edges(zero_ref, range(1, reached - 1), half)
    clear_edges(one_ref, range(reached), half)
    for part in range(2):
        for slot in range(reached):
            layer = layer_of(slot, layers)
            if slot < SWEEPS:
                values = halo_ref[part, jnp.where(on_right, layer - layers, layer + SWEEPS)]
                values = jnp.where(jnp.where(on_right, is_last, is_first), 0.0, values)
            else:
                values = adj_ref[part, layer]
            one_ref[part, slot, pl.ds(PAD, half), :] = values
    for c in (0, 1):
        for layer in range(layers):
            six_ref[c, SWEEPS + layer] = six_own_ref[c, layer]
            cross_ref[c, SWEEPS + layer] = cross_own_ref[c, layer]
    kappa = jnp.broadcast_to(kappa_ref[0:1, :], (rows, size_z))
    for ref, is_near in ((near_cells_ref, True), (far_cells_ref, False)):
        missing = jnp.where(on_right, is_last, is_first)
        if not is_near:
            missing = jnp.where(on_right, is_first, is_last)
        there = jnp.where(missing, 0.0, 1.0)
        for i, (d, c) in enumerate(HALO_CELLS):
            slot = SWEEPS - d if is_near else SWEEPS + layers - 1 + d
            for r in range(0, half, rows):
                six, cross = coefficients(kappa, ref[i, pl.ds(r, rows), :])
                six_ref[c, slot, pl.ds(r, rows), :] = six * there
                cross_ref[c, slot, pl.ds(r, rows), :] = cross * there
    sweeper = Sweeper(half, size_z, layers, source_ref, six_ref, cross_ref)
    sweeper.where[1].update({slot: (one_ref, slot) for slot in range(reached)})
    for k, c in enumerate(COLOURS):
        for slot in range(1 + k, reached - 1 - k):
            sweeper.update(c, slot, (zero_ref, one_ref)[c], slot)


def gradient_terms(slots, zeros, ones, scale_ref, forward_ref, send_ref, keep_ref):
    layers, size_y, size_z = scale_ref.shape
    shards = 2 * send_ref.shape[0]
    shard = lax.axis_index("src")
    shard_rows = size_y // shards
    rows = min(ROWS, shard_rows // 2)
    for slot in slots:
        layer = layer_of(slot, layers)
        swap = odd_lanes(lax.axis_index("tile") * layers + layer, rows, size_z)
        for m in range(shards):
            ref = send_ref if m % 2 else keep_ref
            start = (shard ^ m) * shard_rows
            for r in range(0, shard_rows // 2, rows):
                at = pl.ds(pl.multiple_of(PAD + start // 2 + r, PAD), rows)
                a, b = (
                    [ref[part, i, at, :] for part in range(2)]
                    for ref, i in (zeros[slot], ones[slot])
                )
                for second in range(2):
                    if second:
                        a, b = b, a
                    field = [jnp.where(swap, b[part], a[part]) for part in range(2)]
                    cells = pl.ds(pl.multiple_of(start + 2 * r, 2 * rows) + second, rows, stride=2)
                    products = forward_ref[0, 0, layer, cells, :] * field[1]
                    products += forward_ref[0, 1, layer, cells, :] * field[0]
                    into = pl.ds(2 * r + second, rows, stride=2)
                    ref[m // 2, layer % len(slots), into, :] = (
                        scale_ref[slot - SWEEPS, cells, :] * products
                    )


def far_sweeps(begin, depth, halo_ref, source_ref, six_ref, cross_ref, scale_ref, older, zero_ref, one_ref):
    layers, size_y, size_z = scale_ref.shape
    half = size_y // 2
    tile, tiles = lax.axis_index("tile"), lax.axis_size("tile")
    missing = jnp.where(near_on_right(), tile == 0, tile == tiles - 1)
    bases = (begin - SWEEPS + 1, begin - SWEEPS)
    clear_edges(zero_ref, range(zero_ref.shape[1]), half)
    clear_edges(one_ref, range(one_ref.shape[1]), half)
    for part in range(2):
        for d in range(depth):
            values = jnp.where(missing, 0.0, halo_ref[part, d])
            one_ref[part, begin + d - bases[1], pl.ds(PAD, half), :] = values
    sweeper = Sweeper(half, size_z, layers, source_ref, six_ref, cross_ref)
    for c in (0, 1):
        sweeper.where[c].update(older[c])
    sweeper.where[1].update({begin + d: (one_ref, begin + d - bases[1]) for d in range(depth)})
    for k, c in enumerate(COLOURS):
        for slot in range(begin - 1 - k, begin + depth - 1 - k):
            sweeper.update(c, slot, (zero_ref, one_ref)[c], slot - bases[c])
    return sweeper.where


def near_values(zero_ref, one_ref):
    reached = 2 * SWEEPS
    return (
        {slot: (zero_ref, slot) for slot in range(1, reached - 1)},
        {slot: (one_ref, slot) for slot in range(reached)},
    )


def first_kernel(
    zero_in_ref, one_in_ref, halo_ref, source_ref, six_ref, cross_ref, scale_ref, forward_ref,
    zero_ref, one_ref, send_ref, keep_ref,
):
    depth = halo_ref.shape[1]
    zeros, ones = far_sweeps(
        2 * SWEEPS, depth, halo_ref, source_ref, six_ref, cross_ref, scale_ref,
        near_values(zero_in_ref, one_in_ref), zero_ref, one_ref,
    )
    done = range(SWEEPS, SWEEPS + depth)
    gradient_terms(done, zeros, ones, scale_ref, forward_ref, send_ref, keep_ref)


def second_kernel(
    zero_in_ref, one_in_ref, halo_ref, source_ref, six_ref, cross_ref, scale_ref, forward_ref,
    zero_ref, one_ref, send_ref, keep_ref,
):
    depth = halo_ref.shape[1]
    begin = 2 * SWEEPS + depth
    older = (
        {SWEEPS + 1 + i: (zero_in_ref, i) for i in range(zero_in_ref.shape[1])},
        {SWEEPS + i: (one_in_ref, i) for i in range(one_in_ref.shape[1])},
    )
    zeros, ones = far_sweeps(
        begin, depth, halo_ref, source_ref, six_ref, cross_ref, scale_ref, older, zero_ref, one_ref
    )
    done = range(SWEEPS + depth, SWEEPS + 2 * depth)
    gradient_terms(done, zeros, ones, scale_ref, forward_ref, send_ref, keep_ref)


def unpack_kernel(near_ref, zero_a_ref, one_a_ref, zero_b_ref, one_b_ref, out_hbm, out_ref, sems):
    _, layers, size_y, size_z = out_ref.shape
    depth = layers // 2
    zeros = [(near_ref, SWEEPS)] + [(zero_a_ref, i) for i in range(depth)]
    zeros += [(zero_b_ref, i) for i in range(depth - 1)]
    ones = [(ref, i) for ref in (one_a_ref, one_b_ref) for i in range(depth)]
    half = size_y // 2
    rows = min(ROWS, half)
    first = lax.axis_index("tile") * layers
    copies = []
    for slot in range(SWEEPS, SWEEPS + layers):
        layer = layer_of(slot, layers)
        odd = odd_lanes(first + layer, rows, size_z)
        for part in range(2):
            for r in range(0, half, rows):
                a = zeros[slot - SWEEPS][0][part, zeros[slot - SWEEPS][1], pl.ds(PAD + r, rows), :]
                b = ones[slot - SWEEPS][0][part, ones[slot - SWEEPS][1], pl.ds(PAD + r, rows), :]
                out_ref[part, slot - SWEEPS, pl.ds(2 * r, rows, stride=2), :] = jnp.where(odd, b, a)
                out_ref[part, slot - SWEEPS, pl.ds(2 * r + 1, rows, stride=2), :] = jnp.where(odd, a, b)
        i = slot - SWEEPS
        copies.append(
            pltpu.make_async_copy(out_ref.at[:, i], out_hbm.at[0, :, layer], sems.at[i])
        )
        copies[-1].start()
    for copy in copies:
        copy.wait()


def join_kernel(keep_in_ref, got_ref, send_ref, keep_ref):
    for i in range(keep_in_ref.shape[0]):
        ref = send_ref if i % 2 else keep_ref
        ref[i // 2] = keep_in_ref[i] + got_ref[i]


def finish_kernel(begun_ref, begun_got_ref, ended_ref, ended_got_ref, out_ref):
    depth = begun_ref.shape[1]
    base = jnp.where(near_on_right(), depth, 0)
    for d in range(depth):
        out_ref[base + d] = begun_ref[0, d] + begun_got_ref[0, d]
        out_ref[depth - base + d] = ended_ref[0, d] + ended_got_ref[0, d]


def call(kernel, outs, scratch, specs, out_specs, flops, room=8):
    return pl.pallas_call(
        kernel,
        out_shape=[jax.ShapeDtypeStruct(s, jnp.float32) for s in outs],
        in_specs=specs,
        out_specs=out_specs,
        scratch_shapes=scratch,
        compiler_params=pltpu.CompilerParams(vmem_limit_bytes=room << 20),
        cost_estimate=pl.CostEstimate(flops=flops, bytes_accessed=4 << 20, transcendentals=0),
    )


def in_hbm(array):
    return pltpu.with_memory_space_constraint(array, pltpu.HBM)


def floats(*shapes):
    return [pltpu.VMEM(s, jnp.float32) for s in shapes]


def swaps(jobs, tiles, shards, odd_of, spare):
    pairs = []
    for j in range(jobs):
        for t in range(tiles):
            for s in range(shards):
                other = (t + 1 ^ 1) - 1 if odd_of(s) else t ^ 1
                to = (j, other, s)
                if not 0 <= other < tiles:
                    k, u = spare(j, s)
                    to = (k, t, u)
                to = (to[0] * tiles + to[1]) * shards + to[2]
                pairs.append(((j * tiles + t) * shards + s, to))
    return pairs


def body(
    forward_field,
    adjoint_guess,
    conductivity,
    freq_kappa,
    pair_freq,
    recv_data,
    recv_weights,
    recv_x,
    recv_y,
    recv_z,
):
    pairs, _, layers, size_y, size_z = adjoint_guess.shape
    half = size_y // 2
    count, taps = recv_weights.shape
    tiles = lax.axis_size("tile")
    shards = lax.axis_size("src")
    assert pairs == 1 and layers == SWEEPS and count % UNROLL == 0
    cells = len(HALO_CELLS)
    reach = layers + 2 * (SWEEPS - 1)
    slots = layers + 2 * SWEEPS
    flip = [(i, i ^ 1) for i in range(shards)]

    depth = layers // 2
    piece = (2, depth, half, size_z)
    adj, adj_first, adj_second = call(
        pack_kernel,
        [(2, layers, half, size_z), piece, piece],
        floats((2, layers, size_y, size_z)) + [pltpu.SemaphoreType.DMA((layers,))],
        [HBM],
        [VMEM] * 3,
        1 << 20,
    )(in_hbm(adjoint_guess))
    (cells_out,) = call(
        cells_kernel,
        [(cells, half, size_z)],
        floats((SWEEPS - 1, size_y, size_z)) + [pltpu.SemaphoreType.DMA((1,))],
        [HBM],
        [VMEM],
        1 << 20,
    )(in_hbm(conductivity))
    every = ("job", "tile", "src")
    jobs = lax.axis_size("job")
    unused = (lambda j, s: (j, s ^ 2)) if jobs % 2 else (lambda j, s: (j ^ 1, s))
    to_near = swaps(jobs, tiles, shards, is_even, lambda j, s: (j, s ^ 2))
    to_far = swaps(jobs, tiles, shards, is_odd, unused)
    far_cells = lax.ppermute(cells_out, every, to_far)
    near_halo = lax.ppermute(adj, every, to_near)
    first_halo = lax.ppermute(adj_first, every, to_far)
    second_halo = lax.ppermute(adj_second, every, to_far)

    source, six_own, cross_own, scale, kappa = call(
        source_kernel,
        [
            (2, 2, reach, half, size_z),
            (2, layers, half, size_z),
            (2, layers, half, size_z),
            (layers, size_y, size_z),
            (8, size_z),
        ],
        [pltpu.SMEM((count,), jnp.int32)] * 3
        + [pltpu.SMEM(freq_kappa.shape, jnp.float32)]
        + floats(
            (taps, count),
            recv_data.shape,
            (layers, size_y, size_z),
            (8 * count, size_z),
            (reach + 8, 2 * size_y, size_z),
        )
        + [pltpu.SemaphoreType.DMA((7,))],
        [HBM] * 4 + [SMEM] + [HBM] * 3,
        [VMEM] * 5,
        1 << 30,
        room=16,
    )(
        in_hbm(recv_x), in_hbm(recv_y), in_hbm(recv_z), in_hbm(freq_kappa), pair_freq,
        in_hbm(recv_weights.T), in_hbm(recv_data), in_hbm(conductivity),
    )

    near_cells = lax.ppermute(far_cells, "src", flip)

    state = (2, 2 * SWEEPS, half + 2 * PAD, size_z)
    weights = (2, slots, half, size_z)
    zero, one, six, cross = call(
        near_kernel, [state, state, weights, weights], [], [VMEM] * 8, [VMEM] * 4, 1 << 26
    )(
        adj, near_halo, far_cells, near_cells, source, six_own, cross_own, kappa
    )

    shard_rows = size_y // shards
    part_shape = (shards // 2, depth, shard_rows, size_z)

    state_zero = (2, depth + SWEEPS - 2, half + 2 * PAD, size_z)
    state_one = (2, depth + SWEEPS, half + 2 * PAD, size_z)

    def far(kernel, *values):
        return call(
            kernel,
            [state_zero, state_one, part_shape, part_shape],
            [],
            [VMEM] * 8,
            [VMEM] * 4,
            1 << 26,
        )(*values, source, six, cross, scale, forward_field)

    zero_a, one_a, send_a, keep_a = far(first_kernel, zero, one, first_halo)
    got_b = lax.ppermute(send_a, "src", flip)
    zero_b, one_b, send_b, keep_b = far(second_kernel, zero_a, one_a, second_halo)
    got_a = lax.ppermute(send_b, "src", flip)

    (field,) = call(
        unpack_kernel,
        [(1, 2, layers, size_y, size_z)],
        floats((2, layers, size_y, size_z)) + [pltpu.SemaphoreType.DMA((layers,))],
        [VMEM] * 5,
        [HBM],
        1 << 20,
    )(zero, zero_a, one_a, zero_b, one_b)

    def join(keep, got):
        joined = (shards // 4, depth, shard_rows, size_z)
        return call(join_kernel, [joined, joined], [], [VMEM] * 2, [VMEM] * 2, 1 << 20)(keep, got)

    def add_up(send, keep):
        bit = 2
        while True:
            got = lax.ppermute(send, "src", [(i, i ^ bit) for i in range(shards)])
            bit *= 2
            if bit == shards:
                return keep, got
            keep = keep + got
            send, keep = keep[1::2], keep[0::2]

    ended = add_up(*join(keep_b, got_b))
    begun = add_up(*join(keep_a, got_a))
    (gradient,) = call(
        finish_kernel, [(layers, shard_rows, size_z)], [], [VMEM] * 4, [VMEM], 1 << 20
    )(*begun, *ended)
    return (field, gradient)


def solution(mesh):
    placed = (
        P(("job", "src"), None, "tile", None, None),
        P(("job", "src"), None, "tile", None, None),
        P(("job", "tile"), None, None),
        P("job"),
        P(("job", "src")),
        P(("job", "src"), None, None),
        P("job", None),
        P("job"),
        P("job"),
        P("job"),
    )
    return jax.shard_map(
        body,
        mesh=mesh,
        in_specs=placed,
        out_specs=(P(("job", "src"), None, "tile", None, None), P(("job", "tile"), "src", None)),
        check_vma=False,
    )
```

```python
import jax
import jax.numpy as jnp
from jax import lax
from jax.experimental import pallas as pl
from jax.experimental.pallas import tpu as pltpu
from jax.sharding import PartitionSpec as P


SWEEPS = 4
COLOURS = tuple(k % 2 for k in range(SWEEPS))
HALO_CELLS = tuple(
    (d, c)
    for d in range(1, SWEEPS)
    for c in (0, 1)
    if any(COLOURS[k] == c and d <= SWEEPS - 1 - k for k in range(SWEEPS))
)
PAD = 8
ROWS = 32
UNROLL = 64
SMEM = pl.BlockSpec(memory_space=pltpu.SMEM)
VMEM = pl.BlockSpec(memory_space=pltpu.VMEM)
HBM = pl.BlockSpec(memory_space=pltpu.HBM)


def odd_lanes(shift, rows, cols):
    return ((lax.broadcasted_iota(jnp.int32, (rows, cols), 1) + shift) & 1) == 1


def of_colour(colour, odd, even_rows, odd_rows):
    if colour == 0:
        return jnp.where(odd, odd_rows, even_rows)
    return jnp.where(odd, even_rows, odd_rows)


def coefficients(kappa, conductivity):
    coupling = kappa * conductivity
    inverse = 1.0 / (36.0 + coupling * coupling)
    return 6.0 * inverse, coupling * inverse


def is_odd(shard):
    return shard % 2 == 1


def is_even(shard):
    return shard % 2 == 0


def near_on_right():
    return (lax.axis_index("tile") % 2 == 0) == is_odd(lax.axis_index("src"))


def layer_of(slot, layers):
    ahead = slot - SWEEPS
    return jnp.where(near_on_right(), layers - 1 - ahead, ahead)


def start_all(copies):
    for copy in copies:
        copy.start()
    return copies


def pack_kernel(guess_hbm, adj_ref, first_ref, second_ref, guess_ref, sems):
    _, layers, half, size_z = adj_ref.shape
    rows = min(ROWS, half)
    first = lax.axis_index("tile") * layers
    depth = first_ref.shape[1]
    copies = start_all(
        [
            pltpu.make_async_copy(guess_hbm.at[0, :, i], guess_ref.at[:, i], sems.at[i])
            for i in range(layers)
        ]
    )
    for layer in range(layers):
        odd = odd_lanes(first + layer, rows, size_z)
        copies[layer].wait()
        for part in range(2):
            for r in range(0, half, rows):
                a = guess_ref[part, layer, pl.ds(2 * r, rows, stride=2), :]
                b = guess_ref[part, layer, pl.ds(2 * r + 1, rows, stride=2), :]
                adj_ref[part, layer, pl.ds(r, rows), :] = of_colour(1, odd, a, b)
    for d in range(SWEEPS):
        layer = layer_of(SWEEPS + layers - 1 - d, layers)
        ref = (first_ref, second_ref)[d // depth]
        for part in range(2):
            ref[part, d % depth] = adj_ref[part, layer]


def cells_kernel(cond_hbm, cells_ref, cond_ref, sems):
    layers = cond_hbm.shape[0]
    deep, size_y, size_z = cond_ref.shape
    half = size_y // 2
    rows = min(ROWS, half)
    to_right = jnp.logical_not(near_on_right())
    base = jnp.where(to_right, layers - deep, 0)
    copy = pltpu.make_async_copy(cond_hbm.at[pl.ds(base, deep)], cond_ref, sems.at[0])
    copy.start()
    copy.wait()
    first = lax.axis_index("tile") * layers + base
    for i, (d, c) in enumerate(HALO_CELLS):
        layer = jnp.where(to_right, deep - d, d - 1)
        odd = odd_lanes(first + layer, rows, size_z)
        for r in range(0, half, rows):
            a = cond_ref[layer, pl.ds(2 * r, rows, stride=2), :]
            b = cond_ref[layer, pl.ds(2 * r + 1, rows, stride=2), :]
            cells_ref[i, pl.ds(r, rows), :] = of_colour(c, odd, a, b)


def source_kernel(
    x_hbm, y_hbm, z_hbm, kappas_hbm, freq_ref, weight_hbm, data_hbm, cond_hbm,
    source_ref, six_ref, cross_ref, scale_ref, kappa_ref,
    x_ref, y_ref, z_ref, kappas_ref, weight_ref, data_ref, cond_ref,
    terms_ref, total_ref, sems,
):
    layers, size_y, size_z = cond_ref.shape
    half = size_y // 2
    rows = min(ROWS, half)
    taps, count = weight_ref.shape
    reach = source_ref.shape[2]
    halo = SWEEPS - 1
    first = lax.axis_index("tile") * layers
    copies = start_all(
        [
            pltpu.make_async_copy(a, b, sems.at[i])
            for i, (a, b) in enumerate(
                (
                    (x_hbm, x_ref), (y_hbm, y_ref), (z_hbm, z_ref), (kappas_hbm, kappas_ref),
                    (weight_hbm, weight_ref), (data_hbm, data_ref),
                    (cond_hbm, cond_ref),
                )
            )
        ]
    )
    for layer in range(reach):
        total_ref[4 + layer] = jnp.zeros(total_ref.shape[1:], jnp.float32)
    for copy in copies:
        copy.wait()
    kappa = kappas_ref[freq_ref[0]]
    kappa_ref[...] = jnp.full(kappa_ref.shape, kappa, jnp.float32)

    blank = jnp.zeros((size_z - taps, count), jnp.float32)
    weights = weight_ref[...]
    for c in range(2):
        terms = jnp.concatenate([weights * data_ref[0, c : c + 1, :], blank], axis=0).T
        for b in range(4):
            moved = pltpu.roll(terms, size_z - 4 * b, 1) if b else terms
            terms_ref[pl.ds(2 * b + c, count, stride=8), :] = moved

    lane = lax.broadcasted_iota(jnp.int32, (8, size_z), 1)

    def add_block(r):
        z = z_ref[r]
        base = jnp.clip(x_ref[r] - first + halo, -4, reach) + 4
        row = 2 * y_ref[r]
        inside = (lane - z).astype(jnp.uint32) < 4
        first_tap = pltpu.roll(terms_ref[pl.ds(pl.multiple_of(8 * r, 8), 8), :], z, 1)
        terms = []
        for a in range(4):
            moved = pltpu.roll(first_tap, size_z - 16 * a, 1) if a else first_tap
            terms.append(jnp.where(inside, moved, 0.0))
        old = [total_ref[base + a, pl.ds(row, 8), :] for a in range(4)]
        for a in range(4):
            total_ref[base + a, pl.ds(row, 8), :] = old[a] + terms[a]

    def some_blocks(step, carry):
        for u in range(UNROLL):
            add_block(step * UNROLL + u)
        return carry

    lax.fori_loop(0, count // UNROLL, some_blocks, 0)

    for ahead in range(layers):
        layer = layer_of(SWEEPS + ahead, layers)
        odd = odd_lanes(first + layer, rows, size_z)
        for r in range(0, half, rows):
            a = cond_ref[layer, pl.ds(2 * r, rows, stride=2), :]
            b = cond_ref[layer, pl.ds(2 * r + 1, rows, stride=2), :]
            for c in (0, 1):
                six, cross = coefficients(kappa, of_colour(c, odd, a, b))
                six_ref[c, ahead, pl.ds(r, rows), :] = six
                cross_ref[c, ahead, pl.ds(r, rows), :] = cross
        scale_ref[ahead] = -(kappa * cond_ref[layer])

    def pack_layer(i, carry):
        layer = layer_of(i + 1, layers)
        odd = odd_lanes(first + layer, rows, size_z)
        for part in range(2):
            for r in range(0, half, rows):
                a = total_ref[4 + halo + layer, pl.ds(4 * r + part, rows, stride=4), :]
                b = total_ref[4 + halo + layer, pl.ds(4 * r + 2 + part, rows, stride=4), :]
                for c in (0, 1):
                    source_ref[c, part, i, pl.ds(r, rows), :] = of_colour(c, odd, a, b)
        return carry

    lax.fori_loop(0, reach, pack_layer, 0)


class Sweeper:
    def __init__(self, half, size_z, layers, source, six, cross):
        self.half, self.size_z = half, size_z
        self.source, self.six, self.cross = source, six, cross
        self.where = ({}, {})
        first = lax.axis_index("tile") * layers
        self.rows = min(ROWS, half)
        base = first + jnp.where(near_on_right(), layers - 1, 0)
        self.odd = odd_lanes(base, self.rows, size_z)
        lane = lax.broadcasted_iota(jnp.int32, (self.rows, size_z), 1)
        self.after, self.before = lane > 0, lane < size_z - 1
        near = lax.broadcasted_iota(jnp.int32, (size_z, size_z), 0)
        near = jnp.abs(near - lax.broadcasted_iota(jnp.int32, (size_z, size_z), 1)) <= 1
        near = jnp.where(near, 1.0, 0.0).astype(jnp.bfloat16)
        self.near = jnp.concatenate([near] * 3, axis=0)

    def along_z(self, values):
        high = values.astype(jnp.bfloat16)
        rest = values - high.astype(jnp.float32)
        middle = rest.astype(jnp.bfloat16)
        low = (rest - middle.astype(jnp.float32)).astype(jnp.bfloat16)
        pieces = jnp.concatenate([high, middle, low], axis=1)
        return jnp.dot(pieces, self.near, preferred_element_type=jnp.float32)

    def sums(self, c, part, slot):
        old = self.where[1 - c]
        (here, at_here), (left, at_left), (right, at_right) = old[slot], old[slot - 1], old[slot + 1]
        rows = self.rows
        upto = 0 if part == 0 else self.half // 4
        if upto:
            beside = self.along_z(here[part, at_here, pl.ds(PAD, upto), :])
        out = []
        for r in range(0, self.half, rows):
            above = here[part, at_here, pl.ds(PAD + r + 1, rows), :]
            below = here[part, at_here, pl.ds(PAD + r - 1, rows), :]
            if (slot + c) % 2:
                above, below = below, above
            total = left[part, at_left, pl.ds(PAD + r, rows), :]
            total += right[part, at_right, pl.ds(PAD + r, rows), :]
            total += jnp.where(self.odd, above, below)
            if r < upto:
                total += beside[r : r + rows]
            else:
                centre = here[part, at_here, pl.ds(PAD + r, rows), :]
                total += centre
                total += jnp.where(self.after, pltpu.roll(centre, 1, 1), 0.0)
                total += jnp.where(self.before, pltpu.roll(centre, self.size_z - 1, 1), 0.0)
            out.append(total + self.source[c, part, slot - 1, pl.ds(r, rows), :])
        return out

    def update(self, c, slot, new, index):
        sums = [self.sums(c, part, slot) for part in range(2)]
        for i, r in enumerate(range(0, self.half, self.rows)):
            six = self.six[c, slot, pl.ds(r, self.rows), :]
            cross = self.cross[c, slot, pl.ds(r, self.rows), :]
            at = pl.ds(PAD + r, self.rows)
            new[0, index, at, :] = six * sums[0][i] + cross * sums[1][i]
            new[1, index, at, :] = six * sums[1][i] - cross * sums[0][i]
        self.where[c][slot] = (new, index)


def clear_edges(ref, slots, half):
    edge = jnp.zeros((PAD, ref.shape[-1]), jnp.float32)
    for part in range(2):
        for slot in slots:
            ref[part, slot, pl.ds(0, PAD), :] = edge
            ref[part, slot, pl.ds(PAD + half, PAD), :] = edge


def near_kernel(
    adj_ref, halo_ref, far_cells_ref, near_cells_ref,
    source_ref, six_own_ref, cross_own_ref, kappa_ref,
    zero_ref, one_ref, six_ref, cross_ref,
):
    _, layers, half, size_z = adj_ref.shape
    tile, tiles = lax.axis_index("tile"), lax.axis_size("tile")
    on_right = near_on_right()
    rows = min(ROWS, half)
    reached = layers + SWEEPS
    is_last, is_first = tile == tiles - 1, tile == 0
    clear_edges(zero_ref, range(1, reached - 1), half)
    clear_edges(one_ref, range(reached), half)
    for part in range(2):
        for slot in range(reached):
            layer = layer_of(slot, layers)
            if slot < SWEEPS:
                values = halo_ref[part, jnp.where(on_right, layer - layers, layer + SWEEPS)]
                values = jnp.where(jnp.where(on_right, is_last, is_first), 0.0, values)
            else:
                values = adj_ref[part, layer]
            one_ref[part, slot, pl.ds(PAD, half), :] = values
    for c in (0, 1):
        for layer in range(layers):
            six_ref[c, SWEEPS + layer] = six_own_ref[c, layer]
            cross_ref[c, SWEEPS + layer] = cross_own_ref[c, layer]
    kappa = jnp.broadcast_to(kappa_ref[0:1, :], (rows, size_z))
    for ref, is_near in ((near_cells_ref, True), (far_cells_ref, False)):
        missing = jnp.where(on_right, is_last, is_first)
        if not is_near:
            missing = jnp.where(on_right, is_first, is_last)
        there = jnp.where(missing, 0.0, 1.0)
        for i, (d, c) in enumerate(HALO_CELLS):
            slot = SWEEPS - d if is_near else SWEEPS + layers - 1 + d
            for r in range(0, half, rows):
                six, cross = coefficients(kappa, ref[i, pl.ds(r, rows), :])
                six_ref[c, slot, pl.ds(r, rows), :] = six * there
                cross_ref[c, slot, pl.ds(r, rows), :] = cross * there
    sweeper = Sweeper(half, size_z, layers, source_ref, six_ref, cross_ref)
    sweeper.where[1].update({slot: (one_ref, slot) for slot in range(reached)})
    for k, c in enumerate(COLOURS):
        for slot in range(1 + k, reached - 1 - k):
            sweeper.update(c, slot, (zero_ref, one_ref)[c], slot)


def gradient_terms(slots, zeros, ones, scale_ref, forward_ref, send_ref, keep_ref):
    layers, size_y, size_z = scale_ref.shape
    shards = 2 * send_ref.shape[0]
    shard = lax.axis_index("src")
    shard_rows = size_y // shards
    rows = min(ROWS, shard_rows // 2)
    for slot in slots:
        layer = layer_of(slot, layers)
        swap = odd_lanes(lax.axis_index("tile") * layers + layer, rows, size_z)
        for m in range(shards):
            ref = send_ref if m % 2 else keep_ref
            start = (shard ^ m) * shard_rows
            for r in range(0, shard_rows // 2, rows):
                at = pl.ds(pl.multiple_of(PAD + start // 2 + r, PAD), rows)
                a, b = (
                    [ref[part, i, at, :] for part in range(2)]
                    for ref, i in (zeros[slot], ones[slot])
                )
                for second in range(2):
                    if second:
                        a, b = b, a
                    field = [jnp.where(swap, b[part], a[part]) for part in range(2)]
                    cells = pl.ds(pl.multiple_of(start + 2 * r, 2 * rows) + second, rows, stride=2)
                    products = forward_ref[0, 0, layer, cells, :] * field[1]
                    products += forward_ref[0, 1, layer, cells, :] * field[0]
                    into = pl.ds(2 * r + second, rows, stride=2)
                    ref[m // 2, layer % len(slots), into, :] = (
                        scale_ref[slot - SWEEPS, cells, :] * products
                    )


def far_sweeps(begin, depth, halo_ref, source_ref, six_ref, cross_ref, scale_ref, older, zero_ref, one_ref):
    layers, size_y, size_z = scale_ref.shape
    half = size_y // 2
    tile, tiles = lax.axis_index("tile"), lax.axis_size("tile")
    missing = jnp.where(near_on_right(), tile == 0, tile == tiles - 1)
    bases = (begin - SWEEPS + 1, begin - SWEEPS)
    clear_edges(zero_ref, range(zero_ref.shape[1]), half)
    clear_edges(one_ref, range(one_ref.shape[1]), half)
    for part in range(2):
        for d in range(depth):
            values = jnp.where(missing, 0.0, halo_ref[part, d])
            one_ref[part, begin + d - bases[1], pl.ds(PAD, half), :] = values
    sweeper = Sweeper(half, size_z, layers, source_ref, six_ref, cross_ref)
    for c in (0, 1):
        sweeper.where[c].update(older[c])
    sweeper.where[1].update({begin + d: (one_ref, begin + d - bases[1]) for d in range(depth)})
    for k, c in enumerate(COLOURS):
        for slot in range(begin - 1 - k, begin + depth - 1 - k):
            sweeper.update(c, slot, (zero_ref, one_ref)[c], slot - bases[c])
    return sweeper.where


def near_values(zero_ref, one_ref):
    reached = 2 * SWEEPS
    return (
        {slot: (zero_ref, slot) for slot in range(1, reached - 1)},
        {slot: (one_ref, slot) for slot in range(reached)},
    )


def first_kernel(
    zero_in_ref, one_in_ref, halo_ref, source_ref, six_ref, cross_ref, scale_ref, forward_ref,
    zero_ref, one_ref, send_ref, keep_ref,
):
    depth = halo_ref.shape[1]
    zeros, ones = far_sweeps(
        2 * SWEEPS, depth, halo_ref, source_ref, six_ref, cross_ref, scale_ref,
        near_values(zero_in_ref, one_in_ref), zero_ref, one_ref,
    )
    done = range(SWEEPS, SWEEPS + depth)
    gradient_terms(done, zeros, ones, scale_ref, forward_ref, send_ref, keep_ref)


def second_kernel(
    zero_in_ref, one_in_ref, halo_ref, source_ref, six_ref, cross_ref, scale_ref, forward_ref,
    zero_ref, one_ref, send_ref, keep_ref,
):
    depth = halo_ref.shape[1]
    begin = 2 * SWEEPS + depth
    older = (
        {SWEEPS + 1 + i: (zero_in_ref, i) for i in range(zero_in_ref.shape[1])},
        {SWEEPS + i: (one_in_ref, i) for i in range(one_in_ref.shape[1])},
    )
    zeros, ones = far_sweeps(
        begin, depth, halo_ref, source_ref, six_ref, cross_ref, scale_ref, older, zero_ref, one_ref
    )
    done = range(SWEEPS + depth, SWEEPS + 2 * depth)
    gradient_terms(done, zeros, ones, scale_ref, forward_ref, send_ref, keep_ref)


def unpack_kernel(near_ref, zero_a_ref, one_a_ref, zero_b_ref, one_b_ref, out_hbm, out_ref, sems):
    _, layers, size_y, size_z = out_ref.shape
    depth = layers // 2
    zeros = [(near_ref, SWEEPS)] + [(zero_a_ref, i) for i in range(depth)]
    zeros += [(zero_b_ref, i) for i in range(depth - 1)]
    ones = [(ref, i) for ref in (one_a_ref, one_b_ref) for i in range(depth)]
    half = size_y // 2
    rows = min(ROWS, half)
    first = lax.axis_index("tile") * layers
    copies = []
    for slot in range(SWEEPS, SWEEPS + layers):
        layer = layer_of(slot, layers)
        odd = odd_lanes(first + layer, rows, size_z)
        for part in range(2):
            for r in range(0, half, rows):
                a = zeros[slot - SWEEPS][0][part, zeros[slot - SWEEPS][1], pl.ds(PAD + r, rows), :]
                b = ones[slot - SWEEPS][0][part, ones[slot - SWEEPS][1], pl.ds(PAD + r, rows), :]
                out_ref[part, slot - SWEEPS, pl.ds(2 * r, rows, stride=2), :] = jnp.where(odd, b, a)
                out_ref[part, slot - SWEEPS, pl.ds(2 * r + 1, rows, stride=2), :] = jnp.where(odd, a, b)
        i = slot - SWEEPS
        copies.append(
            pltpu.make_async_copy(out_ref.at[:, i], out_hbm.at[0, :, layer], sems.at[i])
        )
        copies[-1].start()
    for copy in copies:
        copy.wait()


def join_kernel(keep_in_ref, got_ref, send_ref, keep_ref):
    for i in range(keep_in_ref.shape[0]):
        ref = send_ref if i % 2 else keep_ref
        ref[i // 2] = keep_in_ref[i] + got_ref[i]


def finish_kernel(begun_ref, begun_got_ref, ended_ref, ended_got_ref, out_ref):
    depth = begun_ref.shape[1]
    base = jnp.where(near_on_right(), depth, 0)
    for d in range(depth):
        out_ref[base + d] = begun_ref[0, d] + begun_got_ref[0, d]
        out_ref[depth - base + d] = ended_ref[0, d] + ended_got_ref[0, d]


def call(kernel, outs, scratch, specs, out_specs, flops, room=8):
    return pl.pallas_call(
        kernel,
        out_shape=[jax.ShapeDtypeStruct(s, jnp.float32) for s in outs],
        in_specs=specs,
        out_specs=out_specs,
        scratch_shapes=scratch,
        compiler_params=pltpu.CompilerParams(vmem_limit_bytes=room << 20),
        cost_estimate=pl.CostEstimate(flops=flops, bytes_accessed=4 << 20, transcendentals=0),
    )


def in_hbm(array):
    return pltpu.with_memory_space_constraint(array, pltpu.HBM)


def floats(*shapes):
    return [pltpu.VMEM(s, jnp.float32) for s in shapes]


def swaps(jobs, tiles, shards, odd_of, spare):
    pairs = []
    for j in range(jobs):
        for t in range(tiles):
            for s in range(shards):
                other = (t + 1 ^ 1) - 1 if odd_of(s) else t ^ 1
                to = (j, other, s)
                if not 0 <= other < tiles:
                    k, u = spare(j, s)
                    to = (k, t, u)
                to = (to[0] * tiles + to[1]) * shards + to[2]
                pairs.append(((j * tiles + t) * shards + s, to))
    return pairs


def body(
    forward_field,
    adjoint_guess,
    conductivity,
    freq_kappa,
    pair_freq,
    recv_data,
    recv_weights,
    recv_x,
    recv_y,
    recv_z,
):
    pairs, _, layers, size_y, size_z = adjoint_guess.shape
    half = size_y // 2
    count, taps = recv_weights.shape
    tiles = lax.axis_size("tile")
    shards = lax.axis_size("src")
    assert pairs == 1 and layers == SWEEPS and count % UNROLL == 0
    cells = len(HALO_CELLS)
    reach = layers + 2 * (SWEEPS - 1)
    slots = layers + 2 * SWEEPS
    flip = [(i, i ^ 1) for i in range(shards)]

    depth = layers // 2
    piece = (2, depth, half, size_z)
    adj, adj_first, adj_second = call(
        pack_kernel,
        [(2, layers, half, size_z), piece, piece],
        floats((2, layers, size_y, size_z)) + [pltpu.SemaphoreType.DMA((layers,))],
        [HBM],
        [VMEM] * 3,
        1 << 20,
    )(in_hbm(adjoint_guess))
    (cells_out,) = call(
        cells_kernel,
        [(cells, half, size_z)],
        floats((SWEEPS - 1, size_y, size_z)) + [pltpu.SemaphoreType.DMA((1,))],
        [HBM],
        [VMEM],
        1 << 20,
    )(in_hbm(conductivity))
    every = ("job", "tile", "src")
    jobs = lax.axis_size("job")
    unused = (lambda j, s: (j, s ^ 2)) if jobs % 2 else (lambda j, s: (j ^ 1, s))
    to_near = swaps(jobs, tiles, shards, is_even, lambda j, s: (j, s ^ 2))
    to_far = swaps(jobs, tiles, shards, is_odd, unused)
    far_cells = lax.ppermute(cells_out, every, to_far)
    near_halo = lax.ppermute(adj, every, to_near)
    first_halo = lax.ppermute(adj_first, every, to_far)
    second_halo = lax.ppermute(adj_second, every, to_far)

    source, six_own, cross_own, scale, kappa = call(
        source_kernel,
        [
            (2, 2, reach, half, size_z),
            (2, layers, half, size_z),
            (2, layers, half, size_z),
            (layers, size_y, size_z),
            (8, size_z),
        ],
        [pltpu.SMEM((count,), jnp.int32)] * 3
        + [pltpu.SMEM(freq_kappa.shape, jnp.float32)]
        + floats(
            (taps, count),
            recv_data.shape,
            (layers, size_y, size_z),
            (8 * count, size_z),
            (reach + 8, 2 * size_y, size_z),
        )
        + [pltpu.SemaphoreType.DMA((7,))],
        [HBM] * 4 + [SMEM] + [HBM] * 3,
        [VMEM] * 5,
        1 << 30,
        room=16,
    )(
        in_hbm(recv_x), in_hbm(recv_y), in_hbm(recv_z), in_hbm(freq_kappa), pair_freq,
        in_hbm(recv_weights.T), in_hbm(recv_data), in_hbm(conductivity),
    )

    near_cells = lax.ppermute(far_cells, "src", flip)

    state = (2, 2 * SWEEPS, half + 2 * PAD, size_z)
    weights = (2, slots, half, size_z)
    zero, one, six, cross = call(
        near_kernel, [state, state, weights, weights], [], [VMEM] * 8, [VMEM] * 4, 1 << 26
    )(
        adj, near_halo, far_cells, near_cells, source, six_own, cross_own, kappa
    )

    shard_rows = size_y // shards
    part_shape = (shards // 2, depth, shard_rows, size_z)

    state_zero = (2, depth + SWEEPS - 2, half + 2 * PAD, size_z)
    state_one = (2, depth + SWEEPS, half + 2 * PAD, size_z)

    def far(kernel, *values):
        return call(
            kernel,
            [state_zero, state_one, part_shape, part_shape],
            [],
            [VMEM] * 8,
            [VMEM] * 4,
            1 << 26,
        )(*values, source, six, cross, scale, forward_field)

    zero_a, one_a, send_a, keep_a = far(first_kernel, zero, one, first_halo)
    got_b = lax.ppermute(send_a, "src", flip)
    zero_b, one_b, send_b, keep_b = far(second_kernel, zero_a, one_a, second_halo)
    got_a = lax.ppermute(send_b, "src", flip)

    (field,) = call(
        unpack_kernel,
        [(1, 2, layers, size_y, size_z)],
        floats((2, layers, size_y, size_z)) + [pltpu.SemaphoreType.DMA((layers,))],
        [VMEM] * 5,
        [HBM],
        1 << 20,
    )(zero, zero_a, one_a, zero_b, one_b)

    def join(keep, got):
        joined = (shards // 4, depth, shard_rows, size_z)
        return call(join_kernel, [joined, joined], [], [VMEM] * 2, [VMEM] * 2, 1 << 20)(keep, got)

    def add_up(send, keep):
        bit = 2
        while True:
            got = lax.ppermute(send, "src", [(i, i ^ bit) for i in range(shards)])
            bit *= 2
            if bit == shards:
                return keep, got
            keep = keep + got
            send, keep = keep[1::2], keep[0::2]

    ended = add_up(*join(keep_b, got_b))
    begun = add_up(*join(keep_a, got_a))
    (gradient,) = call(
        finish_kernel, [(layers, shard_rows, size_z)], [], [VMEM] * 4, [VMEM], 1 << 20
    )(*begun, *ended)
    return (field, gradient)


def solution(mesh):
    placed = (
        P(("job", "src"), None, "tile", None, None),
        P(("job", "src"), None, "tile", None, None),
        P(("job", "tile"), None, None),
        P("job"),
        P(("job", "src")),
        P(("job", "src"), None, None),
        P("job", None),
        P("job"),
        P("job"),
        P("job"),
    )
    return jax.shard_map(
        body,
        mesh=mesh,
        in_specs=placed,
        out_specs=(P(("job", "src"), None, "tile", None, None), P(("job", "tile"), "src", None)),
        check_vma=False,
    )
```
